128 devices in a mesh: dp: 32 (over z, x, core), mp: 4 (over y).
Axes of the slice: x: 4, y: 4, z: 4, core: 2. Of those that a mesh axis runs over, the one named last changes fastest.
Arguments:
- hidden: bfloat16 [40960, 8192], P('dp', 'mp'), may hold values from -6 to 6
- rewards: float32 [256, 160], P('dp'), may hold values from -4 to 4
- lengths: int32 [256], P('dp'), may hold values from 1 to 160, as said below
- dest_shard: int32 [256], P('dp'), may hold values from 0 to 31, as said below
- source_owner: int32 [256], P('dp'), may hold values from 0 to 31, as said below
- pack_offset: int32 [256], P('dp'), may hold values from 0 to 639, as said below
- segment_ids: int32 [20480], P('dp'), may hold values from 0 to 7, as said below
- norm_gain: float32 [8192], replicated, may hold values from 0.5 to 1.5
- w_query: bfloat16 [8192, 4096], P(None, 'mp'), may hold values from -1 to 1
- w_key: bfloat16 [8192, 512], P(None, 'mp'), may hold values from -1 to 1
- w_value: bfloat16 [8192, 512], P(None, 'mp'), may hold values from -0.0625 to 0.0625
- value_head: float32 [8192], P('mp'), may hold values from -0.0625 to 0.0625
- folded_head: float32 [4096], P('mp'), may hold values from -0.09375 to 0.09375
Outputs:
- values: float32 [256, 160], P('dp')
- advantages: float32 [256, 160], P('dp')
The draws below stay inside these ranges and needn't reach their ends.
Inputs may be any that keep to these rules, and one draw needn't show every extreme that they name: `lengths`: rows of a slot past its rollout's length are unused. Every critic shard holds a rollout of 160 rows. Some owner's 8 rollouts all have 160 rows. `dest_shard`: owner o packs its 8 rollouts on the shards o, o + 1, ..., o + 7, modulo the number of shards, one on each. `source_owner`: shard s packs one rollout from each of the owners s, s - 1, ..., s - 7, modulo the number of shards, in some order, agreeing with dest_shard. `pack_offset`: A shard's packed rollouts lie back to back in the order of their index, each with the length that lengths gives it, and fill all 640 rows. `segment_ids`: each packed row names the index of the packed rollout that holds it, as pack_offset and lengths lay them out.
All inputs are finite; a program needn't handle non-finite values.
Results may differ from the reference program's by a relative error of at most 0.007.
Values may be sent and summed in bfloat16 or wider, within the bound.
A program may use at most 192 MiB of HBM per device.

```python
import math
import jax
import jax.numpy as jnp
from jax import lax

D = 8192
HEADS = 32
KV_HEADS = 4
HD = 128
BATCH = 8
SLOT = 160
PACK = 640
ROLL = 256
ROWS = 40960
N_DP = 32


def packing_plan(key):
    base_key = jax.random.fold_in(key, 11)
    subkeys = jax.random.split(base_key, 5)
    shard_count = ROLL // BATCH
    short_rows = 3 * SLOT
    column_ids = jnp.arange(BATCH, dtype=jnp.int32)[None, :]
    shard_ids = jnp.arange(shard_count, dtype=jnp.int32)[:, None]
    ranking = jax.random.randint(subkeys[0], (shard_count, BATCH), 0, 1 << 20) * BATCH + column_ids
    packed_order = jnp.argsort(ranking, axis=1).astype(jnp.int32)
    inverse_order = jnp.argsort(packed_order, axis=1).astype(jnp.int32)
    cut_ids = jnp.arange(1, short_rows, dtype=jnp.int32)[None, :]
    candidates = jax.random.randint(subkeys[1], (shard_count, short_rows - 1), 0, 1 << 20) * short_rows + cut_ids
    candidates = jnp.where((cut_ids == SLOT) | (cut_ids == 2 * SLOT), 1 << 30, candidates)
    candidates = jnp.where((shard_ids == 0) & (cut_ids == SLOT - 1), -1, candidates)
    chosen = jnp.argsort(candidates, axis=1)[:, :BATCH - 4].astype(jnp.int32) + 1
    fixed_cuts = jnp.concatenate([jnp.full((shard_count, 1), SLOT, jnp.int32), jnp.full((shard_count, 1), 2 * SLOT, jnp.int32)], axis=1)
    cut_points = jnp.sort(jnp.concatenate([chosen, fixed_cuts], axis=1), axis=1)
    bounds = jnp.concatenate([jnp.zeros((shard_count, 1), jnp.int32), cut_points, jnp.full((shard_count, 1), short_rows, jnp.int32)], axis=1)
    short_sizes = bounds[:, 1:] - bounds[:, :-1]
    busy_owner = jax.random.randint(subkeys[4], (), 0, shard_count)
    busy_step = (shard_ids - busy_owner) % shard_count
    busy_column = jnp.take_along_axis(inverse_order, jnp.minimum(busy_step, BATCH - 1), axis=1)
    long_at = jax.random.randint(subkeys[2], (shard_count, 1), 0, BATCH)
    long_at = jnp.where(busy_step < BATCH, busy_column, long_at)
    short_index = jnp.clip(jnp.where(column_ids < long_at, column_ids, column_ids - 1), 0, BATCH - 2)
    packed_sizes = jnp.where(column_ids == long_at, SLOT, jnp.take_along_axis(short_sizes, short_index, axis=1)).astype(jnp.int32)
    offsets = (jnp.cumsum(packed_sizes, axis=1) - packed_sizes).astype(jnp.int32)
    source = (shard_ids - packed_order) % shard_count
    row_ids = jnp.arange(PACK, dtype=jnp.int32)[None, :, None]
    segments = jnp.sum((row_ids >= offsets[:, None, :]).astype(jnp.int32), axis=2) - 1
    owner_rank = jax.random.randint(subkeys[3], (shard_count, BATCH), 0, 1 << 20) * BATCH + column_ids
    owner_order = jnp.argsort(owner_rank, axis=1).astype(jnp.int32)
    destination = (shard_ids + owner_order) % shard_count
    position_in = inverse_order.reshape(-1)[destination * BATCH + owner_order]
    owner_lengths = packed_sizes.reshape(-1)[destination * BATCH + position_in]
    return (owner_lengths.reshape(-1).astype(jnp.int32), destination.reshape(-1).astype(jnp.int32), source.reshape(-1).astype(jnp.int32), offsets.reshape(-1), segments.reshape(-1).astype(jnp.int32))


def draw_lengths(key, part):
    return packing_plan(key)[0]


def draw_dest_shard(key, part):
    return packing_plan(key)[1]


def draw_source_owner(key, part):
    return packing_plan(key)[2]


def draw_pack_offset(key, part):
    return packing_plan(key)[3]


def draw_segment_ids(key, part):
    return packing_plan(key)[4]


def draw_w_key(key, part):
    own_key = jax.random.fold_in(key, 31)
    matrix = jnp.clip(jax.random.normal(own_key, (D, KV_HEADS * HD), jnp.float32), -6.0, 6.0) / math.sqrt(D)
    return jnp.clip(matrix, -1.0, 1.0).astype(jnp.bfloat16)


def draw_w_query(key, part):
    own_key = jax.random.fold_in(key, 37)
    matrix = jnp.clip(jax.random.normal(own_key, (D, HEADS * HD), jnp.float32), -6.0, 6.0) / math.sqrt(D)
    return jnp.clip(matrix, -1.0, 1.0).astype(jnp.bfloat16)


def block_levels(rng, dims, cuts, smallest, high):
    gain, own = 1.0, jax.random.fold_in(rng, 6)
    for position, shards_of in cuts:
        heights = jnp.exp(jax.random.uniform(jax.random.fold_in(own, position), (shards_of,), jnp.float32, smallest / len(cuts), high / len(cuts)))
        gain = gain * jnp.repeat(heights, dims[position] // shards_of).reshape([-1 if axis == position else 1 for axis in range(len(dims))])
    return gain


def centred(key, extent, width, most, pieces=(), held_as=jnp.bfloat16):
    drawn = width * jax.random.normal(key, extent, jnp.float32)
    if pieces:
        drawn = drawn * block_levels(key, extent, pieces, -0.22, 0.18)
    return jnp.clip(drawn, -most, most).astype(held_as)


def setup_inputs(seed: int = 0) -> dict:
    key_list = jax.random.split(jax.random.key(seed), 14)
    hidden = centred(key_list[0], (ROWS, D), 1.0, 6.0, ((0, 32), (1, 4)))
    rewards = centred(key_list[1], (ROLL, SLOT), 0.5, 4.0, ((0, 32),), jnp.float32)
    lengths = draw_lengths(jax.random.fold_in(key_list[13], 71), 0)
    dest_shard = draw_dest_shard(jax.random.fold_in(key_list[13], 71), 0)
    source_owner = draw_source_owner(jax.random.fold_in(key_list[13], 71), 0)
    pack_offset = draw_pack_offset(jax.random.fold_in(key_list[13], 71), 0)
    segment_ids = draw_segment_ids(jax.random.fold_in(key_list[13], 71), 0)
    norm_gain = jnp.clip(1.0 + 0.1 * jax.random.normal(key_list[7], (D,), jnp.float32), 0.5, 1.5)
    w_query = draw_w_query(jax.random.fold_in(key_list[13], 71), 0)
    w_key = draw_w_key(jax.random.fold_in(key_list[13], 71), 0)
    w_value = centred(key_list[10], (D, KV_HEADS * HD), D ** -0.5, 0.0625, ((1, 4),))
    value_head = centred(key_list[11], (D,), D ** -0.5, 0.0625, ((0, 4),), jnp.float32)
    folded_head = centred(key_list[12], (HEADS * HD,), (HEADS * HD) ** -0.5, 0.09375, ((0, 4),), jnp.float32)
    return {"hidden": hidden, "rewards": rewards, "lengths": lengths, "dest_shard": dest_shard, "source_owner": source_owner, "pack_offset": pack_offset, "segment_ids": segment_ids, "norm_gain": norm_gain, "w_query": w_query, "w_key": w_key, "w_value": w_value, "value_head": value_head, "folded_head": folded_head}


EPSILON = 1e-05
DISCOUNT = 0.99
SMOOTHING = 0.95
ROPE_BASE = 500000.0

def rotary(values_in, positions):
    half_width = values_in.shape[-1] // 2
    frequency = ROPE_BASE ** (-jnp.arange(half_width, dtype=jnp.float32) / half_width)
    angles = positions.astype(jnp.float32)[:, None] * frequency[None, :]
    cosine = jnp.cos(angles)[:, None, :]
    sine_part = jnp.sin(angles)[:, None, :]
    front_half = values_in[..., :half_width]
    back_half = values_in[..., half_width:]
    return jnp.concatenate([front_half * cosine - back_half * sine_part, back_half * cosine + front_half * sine_part], axis=-1)

def head_values(queries, keys_out, values_out, segments, positions, folded_head):
    row_count = queries.shape[0]
    kv_count = keys_out.shape[1] // HD
    group_size = queries.shape[1] // HD // kv_count
    query_rot = rotary(queries.reshape(row_count, kv_count * group_size, HD), positions).astype(jnp.bfloat16)
    query_rot = query_rot.reshape(row_count, kv_count, group_size, HD)
    key_rot = rotary(keys_out.reshape(row_count, kv_count, HD), positions).astype(jnp.bfloat16)
    value_rows = values_out.astype(jnp.bfloat16).reshape(row_count, kv_count, HD)
    scores = jnp.einsum('qhgd,khd->hgqk', query_rot.astype(jnp.float32), key_rot.astype(jnp.float32)) / math.sqrt(HD)
    allowed = (segments[:, None] == segments[None, :]) & (positions[:, None] >= positions[None, :])
    scores = jnp.where(allowed[None, None], scores, -1e+30)
    row_max = lax.optimization_barrier(jnp.max(scores, axis=-1, keepdims=True))
    exp_scores = jnp.where(allowed[None, None], jnp.exp(scores - row_max), 0.0)
    row_total = lax.optimization_barrier(jnp.sum(exp_scores, axis=-1, keepdims=True))
    weights = (exp_scores / row_total).astype(jnp.bfloat16)
    attended = jnp.einsum('hgqk,khd->qhgd', weights.astype(jnp.float32), value_rows.astype(jnp.float32))
    return lax.optimization_barrier(jnp.sum(attended.reshape(row_count, -1) * folded_head[None, :], axis=1))

def advantage_of(values, rewards, lengths):
    step_ids = jnp.arange(values.shape[1], dtype=jnp.int32)
    live_mask = step_ids[None, :] < lengths[:, None]
    next_live = step_ids[None, :] + 1 < lengths[:, None]
    following = jnp.concatenate([values[:, 1:], jnp.zeros((values.shape[0], 1), jnp.float32)], axis=1)
    one_step = jnp.where(live_mask, rewards + DISCOUNT * jnp.where(next_live, following, 0.0) - values, 0.0)
    lag_matrix = (step_ids[:, None] - step_ids[None, :]).astype(jnp.float32)
    decay_table = jnp.where(lag_matrix >= 0, jnp.exp(lag_matrix * math.log(DISCOUNT * SMOOTHING)), 0.0)
    return jnp.dot(one_step, decay_table, precision=lax.Precision.HIGHEST)

def reference(hidden, rewards, lengths, dest_shard, source_owner, pack_offset, segment_ids, norm_gain, w_query, w_key, w_value, value_head, folded_head):
    owner_dest = dest_shard.reshape(N_DP, BATCH)
    shard_owner = source_owner.reshape(N_DP, BATCH)
    shard_offset = pack_offset.reshape(N_DP, BATCH)
    shard_segment = segment_ids.reshape(N_DP, PACK)
    slot_lanes = jnp.arange(BATCH, dtype=jnp.int32)

    def one_shard(shard_id):
        owners = shard_owner[shard_id]
        offsets = shard_offset[shard_id]
        segments = shard_segment[shard_id]
        slot_of = lax.optimization_barrier(jnp.sum(jnp.where(owner_dest[owners] == shard_id, slot_lanes[None, :], 0), axis=1)).astype(jnp.int32)
        positions = jnp.arange(PACK, dtype=jnp.int32) - offsets[segments]
        source_rows = ((owners[segments] * BATCH + slot_of[segments]) * SLOT + positions).astype(jnp.int32)
        packed = hidden[source_rows]
        packed_f = packed.astype(jnp.float32)
        row_scale = lax.rsqrt(lax.optimization_barrier(jnp.mean(packed_f * packed_f, axis=1)) + EPSILON)
        normed = (packed_f * row_scale[:, None] * norm_gain[None, :]).astype(jnp.bfloat16)
        queries = jnp.dot(normed, w_query, preferred_element_type=jnp.float32)
        keys_out = jnp.dot(normed, w_key, preferred_element_type=jnp.float32)
        values_out = jnp.dot(normed, w_value, preferred_element_type=jnp.float32)
        attention_term = head_values(queries, keys_out, values_out, segments, positions, folded_head)
        return attention_term + lax.optimization_barrier(jnp.sum(packed_f * value_head[None, :], axis=1))
    packed_values = lax.map(one_shard, jnp.arange(N_DP, dtype=jnp.int32))
    owner_ids = jnp.arange(ROLL, dtype=jnp.int32) // BATCH
    j_of = lax.optimization_barrier(jnp.sum(jnp.where(shard_owner[dest_shard] == owner_ids[:, None], slot_lanes[None, :], 0), axis=1)).astype(jnp.int32)
    start_of = shard_offset[dest_shard, j_of]
    step_ids = jnp.arange(SLOT, dtype=jnp.int32)
    row_index = jnp.minimum(start_of[:, None] + step_ids[None, :], PACK - 1).astype(jnp.int32)
    gathered = packed_values[dest_shard[:, None], row_index]
    values = jnp.where(step_ids[None, :] < lengths[:, None], gathered, 0.0)
    return (values, advantage_of(values, rewards, lengths))
```

```python
import math

import jax
import jax.numpy as jnp
from jax import lax
from jax.sharding import PartitionSpec as P

HD = 128


EPSILON = 1e-05
DISCOUNT = 0.99
SMOOTHING = 0.95
ROPE_BASE = 500000.0


def passed_along(value, axis, by):
    length = lax.axis_size(axis)
    return lax.ppermute(value, axis, [(i, (i + by) % length) for i in range(length)])


def rotary(values_in, positions):
    half_width = values_in.shape[-1] // 2
    frequency = ROPE_BASE ** (-jnp.arange(half_width, dtype=jnp.float32) / half_width)
    angles = positions.astype(jnp.float32)[:, None] * frequency[None, :]
    cosine = jnp.cos(angles)[:, None, :]
    sine_part = jnp.sin(angles)[:, None, :]
    front_half = values_in[..., :half_width]
    back_half = values_in[..., half_width:]
    return jnp.concatenate(
        [front_half * cosine - back_half * sine_part, back_half * cosine + front_half * sine_part],
        axis=-1,
    )


def head_values(queries, keys_out, values_out, segments, positions, folded_head):
    row_count = queries.shape[0]
    kv_count = keys_out.shape[1] // HD
    group_size = queries.shape[1] // HD // kv_count
    query_rot = rotary(queries.reshape(row_count, kv_count * group_size, HD), positions).astype(
        jnp.bfloat16
    )
    query_rot = query_rot.reshape(row_count, kv_count, group_size, HD)
    key_rot = rotary(keys_out.reshape(row_count, kv_count, HD), positions).astype(jnp.bfloat16)
    value_rows = values_out.astype(jnp.bfloat16).reshape(row_count, kv_count, HD)
    scores = jnp.einsum(
        "qhgd,khd->hgqk", query_rot, key_rot, preferred_element_type=jnp.float32
    ) / math.sqrt(HD)
    allowed = (segments[:, None] == segments[None, :]) & (positions[:, None] >= positions[None, :])
    scores = jnp.where(allowed[None, None], scores, -1e30)
    row_max = jnp.max(scores, axis=-1, keepdims=True)
    exp_scores = jnp.where(allowed[None, None], jnp.exp(scores - row_max), 0.0)
    row_total = jnp.sum(exp_scores, axis=-1, keepdims=True)
    weights = (exp_scores / row_total).astype(jnp.bfloat16)
    attended = jnp.einsum("hgqk,khd->qhgd", weights, value_rows, preferred_element_type=jnp.float32)
    return jnp.sum(attended.reshape(row_count, -1) * folded_head[None, :], axis=1)


def local(
    hidden,
    rewards,
    lengths,
    dest_shard,
    source_owner,
    pack_offset,
    segment_ids,
    norm_gain,
    w_query,
    w_key,
    w_value,
    value_head,
    folded_head,
):
    shards = lax.axis_size("dp")
    shard_index = lax.axis_index("dp")
    rollouts = lengths.shape[0]
    slot_rows = rewards.shape[1]
    packed_rows = segment_ids.shape[0]
    slot_lanes = jnp.arange(rollouts, dtype=jnp.int32)

    def slot_for(shift_by):
        target = (shard_index + shift_by) % shards
        return jnp.sum(jnp.where(dest_shard == target, slot_lanes, 0))

    def outgoing(shift_by, source):
        return lax.dynamic_slice_in_dim(source, slot_for(shift_by) * slot_rows, slot_rows, 0)

    source_step = (shard_index - source_owner) % shards
    lane_match = segment_ids[:, None] == slot_lanes[None, :]
    row_step = jnp.sum(jnp.where(lane_match, source_step[None, :], 0), axis=1)
    row_offset = jnp.sum(jnp.where(lane_match, pack_offset[None, :], 0), axis=1)
    positions = jnp.arange(packed_rows, dtype=jnp.int32) - row_offset
    pick_rows = row_step * slot_rows + positions
    received = [outgoing(0, hidden)]
    for shift_by in range(1, rollouts):
        received.append(passed_along(outgoing(shift_by, hidden), "dp", shift_by))
    own_part = jnp.take(jnp.concatenate(received, axis=0), pick_rows, axis=0)
    packed = lax.all_gather(own_part, "mp", axis=1, tiled=True)
    packed_f = packed.astype(jnp.float32)
    row_scale = lax.rsqrt(jnp.mean(packed_f * packed_f, axis=1) + EPSILON)
    normed = (packed_f * row_scale[:, None] * norm_gain[None, :]).astype(jnp.bfloat16)
    queries = jnp.dot(normed, w_query, preferred_element_type=jnp.float32)
    keys_out = jnp.dot(normed, w_key, preferred_element_type=jnp.float32)
    values_out = jnp.dot(normed, w_value, preferred_element_type=jnp.float32)
    value_terms = head_values(queries, keys_out, values_out, segment_ids, positions, folded_head)
    value_terms = value_terms + jnp.sum(own_part.astype(jnp.float32) * value_head[None, :], axis=1)
    packed_values = lax.psum(value_terms, "mp")
    padded = jnp.concatenate([packed_values, jnp.zeros((slot_rows,), jnp.float32)])
    slot_values = jnp.zeros((rollouts, slot_rows), jnp.float32)
    for shift_by in range(rollouts):
        owner_now = (shard_index - shift_by) % shards
        j_index = jnp.sum(jnp.where(source_owner == owner_now, slot_lanes, 0))
        start_at = jnp.sum(jnp.where(slot_lanes == j_index, pack_offset, 0))
        arrived = lax.dynamic_slice_in_dim(padded, start_at, slot_rows, 0)
        if shift_by:
            arrived = passed_along(arrived, "dp", -shift_by)
        slot_values = jnp.where(
            (slot_lanes == slot_for(shift_by))[:, None], arrived[None, :], slot_values
        )
    step_ids = jnp.arange(slot_rows, dtype=jnp.int32)
    live_mask = step_ids[None, :] < lengths[:, None]
    values = jnp.where(live_mask, slot_values, 0.0)
    next_live = step_ids[None, :] + 1 < lengths[:, None]
    following = jnp.concatenate([values[:, 1:], jnp.zeros((rollouts, 1), jnp.float32)], axis=1)
    one_step = jnp.where(
        live_mask, rewards + DISCOUNT * jnp.where(next_live, following, 0.0) - values, 0.0
    )
    lag_matrix = (step_ids[:, None] - step_ids[None, :]).astype(jnp.float32)
    decay_table = jnp.where(
        lag_matrix >= 0, jnp.exp(lag_matrix * math.log(DISCOUNT * SMOOTHING)), 0.0
    )
    advantages = jnp.dot(one_step, decay_table, precision=lax.Precision.HIGHEST)
    return (values, advantages)


def solution(mesh):
    return jax.shard_map(
        local,
        mesh=mesh,
        in_specs=(
            P("dp", "mp"),
            P("dp", None),
            P("dp"),
            P("dp"),
            P("dp"),
            P("dp"),
            P("dp"),
            P(),
            P(None, "mp"),
            P(None, "mp"),
            P(None, "mp"),
            P("mp"),
            P("mp"),
        ),
        out_specs=(P("dp", None), P("dp", None)),
        check_vma=False,
    )
```

```python
import math

import jax
import jax.numpy as jnp
import numpy as np
from jax import lax
from jax.experimental import pallas as pl
from jax.experimental.pallas import tpu as pltpu
from jax.sharding import PartitionSpec as P

MESH = pl.DeviceIdType.MESH
F32 = jnp.float32
BF16 = jnp.bfloat16

HD = 128
EPSILON = 1e-05
DISCOUNT = 0.99
SMOOTHING = 0.95
ROPE_BASE = 500000.0

SHARDS = 32
PLANES = 4
STEPS = 8
SLOT = 160
PACK = 640
TILE = 128
TILES = PACK // TILE
WIDTH = 256
CHUNKS = 8
HEADS = 8
COLS = HEADS * HD + 2 * HD
BAND = SLOT + TILE
LANES = 256
BEFORE = 4
HALF = PACK // 2
PLANE_OF = (0, -1, 1, 2)

CONTRACT_LAST = (((1,), (1,)), ((), ()))


def dot_last(a, b):
    return lax.dot_general(a, b, CONTRACT_LAST, preferred_element_type=F32)


def thirds(value):
    high = value.astype(BF16)
    rest = value - high.astype(F32)
    middle = rest.astype(BF16)
    return high, middle, (rest - middle.astype(F32)).astype(BF16)


def wide_row(ref, row):
    return jnp.concatenate([ref[pl.ds(2 * row + i, 1), :] for i in range(2)], axis=1)


def sum_of_thirds(stacked):
    rows = stacked.shape[0] // 3
    return stacked[:rows] + stacked[rows : 2 * rows] + stacked[2 * rows :]


def kernel(
    lengths,
    dest_shard,
    source_owner,
    pack_offset,
    segments,
    gain,
    value_head,
    folded_head,
    frequency,
    rewards,
    hidden,
    w_query,
    w_key,
    w_value,
    values_out,
    advantages_out,
    first_slots,
    slots,
    outbox,
    inbox,
    weights,
    rows,
    total,
    squares,
    head_terms,
    select,
    cosines,
    sines,
    picks_out,
    picks,
    query_rot,
    key_rot,
    value_rows,
    packed_values,
    by_plane,
    by_step,
    arrived,
    padded_rewards,
    slot_sem,
    weight_sem,
    pick_sem,
    send_sem,
    recv_sem,
    ring_send,
    ring_recv,
    pass_send,
    pass_recv,
    plane_send,
    plane_recv,
    back_send,
    back_recv,
):
    dp = lax.axis_index("dp")
    mp = lax.axis_index("mp")

    def along_dp(by):
        return lax.rem(dp + (by + SHARDS), SHARDS), mp

    def along_mp(by):
        return dp, lax.rem(mp + (by + PLANES), PLANES)

    barrier = pltpu.get_barrier_semaphore()
    peers = [along_dp(by) for by in range(-BEFORE, BEFORE + 1) if by]
    peers += [along_mp(by) for by in (1, -1, 2)]
    for peer in peers:
        pl.semaphore_signal(barrier, inc=1, device_id=peer, device_id_type=MESH)

    def slot_copy(chunk):
        columns = pl.ds(chunk * WIDTH, WIDTH)
        target = first_slots if chunk == 0 else slots.at[chunk - 1]
        return pltpu.make_async_copy(hidden.at[:, :, columns], target, slot_sem.at[chunk])

    weight_copies = [
        pltpu.make_async_copy(source, weights.at[:, :, pl.ds(start, source.shape[2])], weight_sem.at[i])
        for i, (source, start) in enumerate(
            ((w_query, 0), (w_key, HEADS * HD), (w_value, HEADS * HD + HD))
        )
    ]
    for chunk in range(CHUNKS):
        slot_copy(chunk).start()
    for copy in weight_copies:
        copy.start()

    sublanes = lax.broadcasted_iota(jnp.int32, (TILES, TILE), 0)
    lanes = lax.broadcasted_iota(jnp.int32, (TILES, TILE), 1)
    pick = sublanes * TILE + lanes
    segment = segments[...]
    for j in range(STEPS):
        step = lax.rem(dp - source_owner[j] + SHARDS, SHARDS)
        pick = pick + jnp.where(segment == j, step * SLOT - pack_offset[j], 0)
    picks_out[0:TILES, :] = pick
    picks_out[TILES:, :] = jnp.zeros((8 - TILES, TILE), jnp.int32)

    slot_of = []
    for k in range(STEPS):
        shard = lax.rem(dp + k, SHARDS)
        slot = jnp.int32(0)
        for i in range(STEPS):
            slot = jnp.maximum(slot, jnp.where(dest_shard[i] == shard, i, 0))
        slot_of.append(slot)

    def send_copy(chunk, k):
        return pltpu.make_async_remote_copy(
            src_ref=outbox.at[chunk, k],
            dst_ref=inbox.at[chunk, pl.ds(k * SLOT, SLOT)],
            send_sem=send_sem.at[chunk, k],
            recv_sem=recv_sem.at[chunk, k],
            device_id=along_dp(k - BEFORE),
            device_id_type=MESH,
        )

    others = [k for k in range(STEPS) if k != BEFORE]

    def order_slots(chunk, load):
        for k in range(STEPS):
            if k == BEFORE:
                inbox[chunk, k * SLOT : (k + 1) * SLOT, :] = load(slot_of[k])
            else:
                outbox[chunk, k] = load(slot_of[k])

    slot_copy(0).wait()
    order_slots(0, lambda slot: first_slots[slot])

    pl.semaphore_wait(barrier, len(peers))

    pick_copy = pltpu.make_async_remote_copy(
        src_ref=picks_out,
        dst_ref=picks,
        send_sem=pick_sem.at[0],
        recv_sem=pick_sem.at[1],
        device_id=along_dp(-BEFORE),
        device_id_type=MESH,
    )
    pick_copy.start()
    for k in others:
        send_copy(0, k).start()
    for chunk in range(1, CHUNKS):
        slot_copy(chunk).wait()

    def send_chunk(chunk, carry):
        order_slots(chunk, lambda slot: slots[chunk - 1, slot])
        for k in others:
            send_copy(chunk, k).start()
        return carry

    lax.fori_loop(1, CHUNKS, send_chunk, 0)

    total[...] = jnp.zeros_like(total)
    squares[...] = jnp.zeros_like(squares)
    head_terms[...] = jnp.zeros_like(head_terms)
    key_rot[0:SLOT, :] = jnp.zeros((SLOT, HD), BF16)
    value_rows[0:SLOT, :] = jnp.zeros((SLOT, HD), BF16)

    pick_copy.wait_recv()
    tile_lanes = lax.broadcasted_iota(jnp.int32, (TILE, TILE), 1)

    def tables(b, carry):
        row = picks[pl.ds(b, 1), :].astype(F32)
        column = jnp.transpose(jnp.broadcast_to(row, (TILE, TILE)))
        at = pl.ds(pl.multiple_of(b * TILE, TILE), TILE)
        for block in range(STEPS * SLOT // TILE):
            hit = column == (tile_lanes + block * TILE).astype(F32)
            select[at, block * TILE : (block + 1) * TILE] = jnp.where(hit, 1.0, 0.0).astype(BF16)
        position = column
        for k in range(1, STEPS):
            position = position - jnp.where(column >= float(k * SLOT), float(SLOT), 0.0)
        angle = position * frequency[...]
        cosines[at, :] = jnp.cos(angle)
        sines[at, :] = jnp.sin(angle) * jnp.where(tile_lanes < HD // 2, -1.0, 1.0)
        return carry

    lax.fori_loop(0, TILES, tables, 0)

    def ring_copy(way, chunk):
        return pltpu.make_async_remote_copy(
            src_ref=rows.at[0, chunk],
            dst_ref=rows.at[1 + way, chunk],
            send_sem=ring_send.at[way, chunk],
            recv_sem=ring_recv.at[way, chunk],
            device_id=along_mp(1 - 2 * way),
            device_id_type=MESH,
        )

    def pass_copy(way, chunk):
        half = pl.ds(way * HALF, HALF)
        return pltpu.make_async_remote_copy(
            src_ref=rows.at[1 + way, chunk, half],
            dst_ref=rows.at[3, chunk, half],
            send_sem=pass_send.at[way, chunk],
            recv_sem=pass_recv.at[way, chunk],
            device_id=along_mp(1 - 2 * way),
            device_id_type=MESH,
        )

    def pack(chunk):
        for k in others:
            send_copy(chunk, k).wait_recv()
        packed = jnp.dot(select[...], inbox[chunk], preferred_element_type=F32).astype(BF16)
        rows[0, chunk] = packed
        parts = thirds(wide_row(value_head, chunk))
        sub = lax.broadcasted_iota(jnp.int32, (8, WIDTH), 0)
        stacked = jnp.zeros((8, WIDTH), F32)
        for i, part in enumerate(parts):
            stacked = jnp.where(sub == i, part.astype(F32), stacked)
        head_terms[...] += dot_last(stacked.astype(BF16), packed)

    def project(part, plane, chunk):
        block = plane * CHUNKS + chunk
        x = rows[part, chunk].astype(F32)
        squared = x * x
        squares[...] += squared[:, :128] + squared[:, 128:]
        scaled = (x * wide_row(gain, block)).astype(BF16)
        for n in range(COLS // WIDTH):
            columns = slice(n * WIDTH, (n + 1) * WIDTH)
            total[:, columns] += jnp.dot(
                scaled, weights[block, :, columns], preferred_element_type=F32
            )

    def advance(t, carry):
        @pl.when(t < CHUNKS)
        def _():
            pack(t)
            ring_copy(0, t).start()
            ring_copy(1, t).start()

        @pl.when(t == 1)
        def _():
            for copy in weight_copies:
                copy.wait()

        @pl.when((t >= 1) & (t <= CHUNKS))
        def _():
            chunk = t - 1
            for way in range(2):
                ring_copy(way, chunk).wait_recv()
                pass_copy(way, chunk).start()

            def near(part, inner):
                plane = lax.rem(mp + part * (3 * part - 5) // 2 + PLANES, PLANES)
                project(part, plane, chunk)
                return inner

            lax.fori_loop(0, 3, near, 0)

        @pl.when(t >= 2)
        def _():
            chunk = t - 2
            for way in range(2):
                pass_copy(way, chunk).wait_recv()
            project(3, lax.rem(mp + 2, PLANES), chunk)

        return carry

    lax.fori_loop(0, CHUNKS + 2, advance, 0)

    query_scale = math.log2(math.e) / math.sqrt(HD)

    def rotate(b, carry):
        at = pl.ds(pl.multiple_of(b * TILE, TILE), TILE)
        below = pl.ds(pl.multiple_of(SLOT + b * TILE, 32), TILE)
        mean = jnp.sum(squares[at, :], axis=1, keepdims=True) / (PLANES * CHUNKS * WIDTH)
        scale = lax.rsqrt(mean + EPSILON)
        cosine, sine = cosines[at, :], sines[at, :]

        def turned(head):
            x = total[at, head * HD : (head + 1) * HD] * scale
            return x * cosine + pltpu.roll(x, HD // 2, 1) * sine

        for head in range(HEADS):
            query_rot[b, head * TILE : (head + 1) * TILE, :] = (turned(head) * query_scale).astype(BF16)
        key_rot[below, :] = turned(HEADS).astype(BF16)
        value_rows[below, :] = (total[at, (HEADS + 1) * HD :] * scale).astype(BF16)
        return carry

    lax.fori_loop(0, TILES, rotate, 0)

    folded = jnp.concatenate([part.astype(F32) for part in thirds(folded_head[...])], axis=0).astype(BF16)
    reach = lax.broadcasted_iota(jnp.int32, (BAND, 2 * TILE), 0) - SLOT
    query_at = lax.rem(lax.broadcasted_iota(jnp.int32, (BAND, 2 * TILE), 1), TILE)
    lane = lax.broadcasted_iota(jnp.int32, (1, TILE), 1)
    step_sub = lax.broadcasted_iota(jnp.int32, (STEPS, TILE), 0)
    time_sub = lax.broadcasted_iota(jnp.int32, (LANES, TILE), 0)
    packed_values[...] = jnp.zeros_like(packed_values)

    def attend(b, carry):
        band = pl.ds(pl.multiple_of(b * TILE, TILE), BAND)
        keys = key_rot[band, :]
        pick_row = picks[pl.ds(b, 1), :]
        step_row = jnp.zeros_like(pick_row)
        for k in range(1, STEPS):
            step_row = step_row + jnp.where(pick_row >= k * SLOT, 1, 0)
        position_row = pick_row - step_row * SLOT
        first = lane - position_row
        first = jnp.concatenate([first, first], axis=1)
        allowed = (reach <= query_at) & (reach >= first)
        through = sum_of_thirds(dot_last(folded, value_rows[band, :]))
        high, low, _ = thirds(through)
        lifted = jnp.concatenate(
            [high.astype(F32), low.astype(F32), jnp.ones((HEADS, BAND), F32)], axis=0
        ).astype(BF16)
        term = jnp.zeros((1, TILE), F32)
        for pair in range(HEADS // 2):
            scores = dot_last(keys, query_rot[b, pair * 2 * TILE : (pair + 1) * 2 * TILE, :])
            scores = jnp.where(allowed, scores, -1e30)
            peak = jnp.max(scores, axis=0, keepdims=True)
            weight = jnp.exp2(scores - peak).astype(BF16)
            sums = jnp.dot(lifted, weight, preferred_element_type=F32)
            for i in range(2):
                head, part = 2 * pair + i, slice(i * TILE, (i + 1) * TILE)
                above = sums[head : head + 1, part] + sums[HEADS + head : HEADS + head + 1, part]
                term = term + above / sums[2 * HEADS : 2 * HEADS + 1, part]
        ends = head_terms[:, pl.ds(pl.multiple_of(b * TILE, TILE), TILE)]
        term = term + (ends[0:1] + ends[1:2] + ends[2:3])
        spread = jnp.where(step_sub == step_row, term, 0.0)
        spread = jnp.concatenate([part.astype(F32) for part in thirds(spread)], axis=0).astype(BF16)
        placed = jnp.where(time_sub == position_row, 1.0, 0.0).astype(BF16)
        packed_values[...] += sum_of_thirds(dot_last(spread, placed))
        return carry

    lax.fori_loop(0, TILES, attend, 0)

    by_plane[mp] = packed_values[...]

    def plane_copy(by):
        return pltpu.make_async_remote_copy(
            src_ref=by_plane.at[mp],
            dst_ref=by_plane.at[mp],
            send_sem=plane_send.at[by - 1],
            recv_sem=plane_recv.at[by - 1],
            device_id=along_mp(by),
            device_id_type=MESH,
        )

    def plane_arrival(by):
        other = along_mp(-by)[1]
        return pltpu.make_async_remote_copy(
            src_ref=by_plane.at[other],
            dst_ref=by_plane.at[other],
            send_sem=plane_send.at[by - 1],
            recv_sem=plane_recv.at[by - 1],
            device_id=along_mp(by),
            device_id_type=MESH,
        )

    for by in range(1, PLANES):
        plane_copy(by).start()
    padded_rewards[...] = jnp.zeros_like(padded_rewards)
    padded_rewards[:, 0:SLOT] = rewards[...]
    for by in range(1, PLANES):
        plane_arrival(by).wait_recv()
    summed = (by_plane[0] + by_plane[1]) + (by_plane[2] + by_plane[3])

    def back_copy(k):
        return pltpu.make_async_remote_copy(
            src_ref=by_step.at[k],
            dst_ref=arrived.at[k],
            send_sem=back_send.at[k],
            recv_sem=back_recv.at[k],
            device_id=along_dp(BEFORE - k),
            device_id_type=MESH,
        )

    for k in range(STEPS):
        one = jnp.broadcast_to(summed[k : k + 1, :], (8, LANES))
        if k == BEFORE:
            arrived[k] = one
        else:
            by_step[k] = one
    for k in others:
        back_copy(k).start()
    for k in others:
        back_copy(k).wait_recv()

    sub = lax.broadcasted_iota(jnp.int32, (STEPS, LANES), 0)
    time = lax.broadcasted_iota(jnp.int32, (STEPS, LANES), 1)
    slot_values = jnp.zeros((STEPS, LANES), F32)
    length = jnp.zeros((STEPS, LANES), jnp.int32)
    for i in range(STEPS):
        step = jnp.minimum(lax.rem(dest_shard[i] - dp + SHARDS, SHARDS), STEPS - 1)
        slot_values = jnp.where(sub == i, arrived[step], slot_values)
        length = jnp.where(sub == i, lengths[i], length)
    live = time < length
    values = jnp.where(live, slot_values, 0.0)
    following = jnp.where(time + 1 < length, pltpu.roll(values, LANES - 1, 1), 0.0)
    advantages = jnp.where(live, padded_rewards[...] + DISCOUNT * following - values, 0.0)
    shift = 1
    while shift < SLOT:
        later = jnp.where(time < LANES - shift, pltpu.roll(advantages, LANES - shift, 1), 0.0)
        advantages = advantages + (DISCOUNT * SMOOTHING) ** shift * later
        shift *= 2
    values_out[...] = values[:, 0:SLOT]
    advantages_out[...] = advantages[:, 0:SLOT]

    pick_copy.wait_send()

    def drain(chunk, carry):
        for k in others:
            send_copy(chunk, k).wait_send()
        for way in range(2):
            ring_copy(way, chunk).wait_send()
            pass_copy(way, chunk).wait_send()
        return carry

    lax.fori_loop(0, CHUNKS, drain, 0)
    for by in range(1, PLANES):
        plane_copy(by).wait_send()
    for k in others:
        back_copy(k).wait_send()


def local(
    hidden,
    rewards,
    lengths,
    dest_shard,
    source_owner,
    pack_offset,
    segment_ids,
    norm_gain,
    w_query,
    w_key,
    w_value,
    value_head,
    folded_head,
):
    blocks = PLANES * CHUNKS
    half = HD // 2
    frequency = (ROPE_BASE ** (-np.arange(half, dtype=np.float64) / half)).astype(np.float32)
    frequency = jnp.asarray(np.concatenate([frequency, frequency])[None, :])
    smem = pl.BlockSpec(memory_space=pltpu.SMEM)
    vmem = pl.BlockSpec(memory_space=pltpu.VMEM)
    hbm = pl.BlockSpec(memory_space=pl.ANY)
    dma = pltpu.SemaphoreType.DMA
    out = jax.ShapeDtypeStruct((STEPS, SLOT), F32)
    return pl.pallas_call(
        kernel,
        name="critic",
        out_shape=(out, out),
        in_specs=[smem] * 4 + [vmem] * 6 + [hbm] * 4,
        out_specs=(vmem, vmem),
        scratch_shapes=[
            pltpu.VMEM((STEPS, SLOT, WIDTH), BF16),
            pltpu.VMEM((CHUNKS - 1, STEPS, SLOT, WIDTH), BF16),
            pltpu.VMEM((CHUNKS, STEPS, SLOT, WIDTH), BF16),
            pltpu.VMEM((CHUNKS, STEPS * SLOT, WIDTH), BF16),
            pltpu.VMEM((blocks, WIDTH, COLS), BF16),
            pltpu.VMEM((PLANES, CHUNKS, PACK, WIDTH), BF16),
            pltpu.VMEM((PACK, COLS), F32),
            pltpu.VMEM((PACK, 128), F32),
            pltpu.VMEM((8, PACK), F32),
            pltpu.VMEM((PACK, STEPS * SLOT), BF16),
            pltpu.VMEM((PACK, HD), F32),
            pltpu.VMEM((PACK, HD), F32),
            pltpu.VMEM((8, TILE), jnp.int32),
            pltpu.VMEM((8, TILE), jnp.int32),
            pltpu.VMEM((TILES, HEADS * TILE, HD), BF16),
            pltpu.VMEM((SLOT + PACK, HD), BF16),
            pltpu.VMEM((SLOT + PACK, HD), BF16),
            pltpu.VMEM((STEPS, LANES), F32),
            pltpu.VMEM((PLANES, STEPS, LANES), F32),
            pltpu.VMEM((STEPS, 8, LANES), F32),
            pltpu.VMEM((STEPS, 8, LANES), F32),
            pltpu.VMEM((STEPS, LANES), F32),
            dma((CHUNKS,)),
            dma((3,)),
            dma((2,)),
            dma((CHUNKS, STEPS)),
            dma((CHUNKS, STEPS)),
            dma((2, CHUNKS)),
            dma((2, CHUNKS)),
            dma((2, CHUNKS)),
            dma((2, CHUNKS)),
            dma((3,)),
            dma((3,)),
            dma((STEPS,)),
            dma((STEPS,)),
        ],
        compiler_params=pltpu.CompilerParams(
            collective_id=0, has_side_effects=True, vmem_limit_bytes=67_043_328
        ),
    )(
        lengths,
        dest_shard,
        source_owner,
        pack_offset,
        segment_ids.reshape(TILES, TILE),
        norm_gain.reshape(2 * blocks, 128),
        value_head.reshape(2 * CHUNKS, 128),
        folded_head.reshape(HEADS, HD),
        frequency,
        rewards,
        hidden.reshape(STEPS, SLOT, CHUNKS * WIDTH),
        w_query.reshape(blocks, WIDTH, HEADS * HD),
        w_key.reshape(blocks, WIDTH, HD),
        w_value.reshape(blocks, WIDTH, HD),
    )


def solution(mesh):
    return jax.shard_map(
        local,
        mesh=mesh,
        in_specs=(
            P("dp", "mp"),
            P("dp", None),
            P("dp"),
            P("dp"),
            P("dp"),
            P("dp"),
            P("dp"),
            P(),
            P(None, "mp"),
            P(None, "mp"),
            P(None, "mp"),
            P("mp"),
            P("mp"),
        ),
        out_specs=(P("dp", None), P("dp", None)),
        check_vma=False,
    )
```

```python
import math

import jax
import jax.numpy as jnp
import numpy as np
from jax import lax
from jax.experimental import pallas as pl
from jax.experimental.pallas import tpu as pltpu
from jax.sharding import PartitionSpec as P

MESH = pl.DeviceIdType.MESH
F32 = jnp.float32
BF16 = jnp.bfloat16

HD = 128
EPSILON = 1e-05
DISCOUNT = 0.99
SMOOTHING = 0.95
ROPE_BASE = 500000.0

SHARDS = 32
PLANES = 4
STEPS = 8
SLOT = 160
PACK = 640
TILE = 128
TILES = PACK // TILE
WIDTH = 256
CHUNKS = 8
HEADS = 8
COLS = HEADS * HD + 2 * HD
BAND = SLOT + TILE
LANES = 256
BEFORE = 4
HALF = PACK // 2


CONTRACT_LAST = (((1,), (1,)), ((), ()))


def dot_last(a, b):
    return lax.dot_general(a, b, CONTRACT_LAST, preferred_element_type=F32)


def thirds(value):
    high = value.astype(BF16)
    rest = value - high.astype(F32)
    middle = rest.astype(BF16)
    return high, middle, (rest - middle.astype(F32)).astype(BF16)


def wide_row(ref, row):
    return jnp.concatenate([ref[pl.ds(2 * row + i, 1), :] for i in range(2)], axis=1)


def sum_of_thirds(stacked):
    rows = stacked.shape[0] // 3
    return stacked[:rows] + stacked[rows : 2 * rows] + stacked[2 * rows :]


def kernel(
    lengths,
    dest_shard,
    gain,
    value_head,
    folded_head,
    frequency,
    rewards,
    hidden,
    w_query,
    w_key,
    w_value,
    both_out,
    first_slots,
    slots,
    outbox,
    inbox,
    weights,
    rows,
    total,
    squares,
    head_terms,
    select,
    cosines,
    sines,
    sizes_out,
    sizes,
    query_rot,
    key_rot,
    value_rows,
    by_plane,
    by_step,
    arrived,
    padded_rewards,
    slot_sem,
    weight_sem,
    size_send,
    size_recv,
    send_sem,
    recv_sem,
    ring_send,
    ring_recv,
    pass_send,
    pass_recv,
    plane_send,
    plane_recv,
    back_send,
    back_recv,
):
    dp = lax.axis_index("dp")
    mp = lax.axis_index("mp")

    def along_dp(by):
        return lax.rem(dp + (by + SHARDS), SHARDS), mp

    def along_mp(by):
        return dp, lax.rem(mp + (by + PLANES), PLANES)

    barrier = pltpu.get_barrier_semaphore()
    peers = [along_dp(by) for by in range(-BEFORE, BEFORE + 1) if by]
    peers += [along_mp(by) for by in (1, -1, 2)]
    for peer in peers:
        pl.semaphore_signal(barrier, inc=1, device_id=peer, device_id_type=MESH)

    def slot_copy(chunk):
        columns = pl.ds(chunk * WIDTH, WIDTH)
        target = first_slots if chunk == 0 else slots.at[chunk - 1]
        return pltpu.make_async_copy(hidden.at[:, :, columns], target, slot_sem.at[chunk])

    weight_copies = [
        pltpu.make_async_copy(source, weights.at[:, :, pl.ds(start, source.shape[2])], weight_sem.at[i])
        for i, (source, start) in enumerate(
            ((w_query, 0), (w_key, HEADS * HD), (w_value, HEADS * HD + HD))
        )
    ]
    for chunk in range(CHUNKS):
        slot_copy(chunk).start()
    for copy in weight_copies:
        copy.start()

    slot_of = []
    for k in range(STEPS):
        shard = lax.rem(dp + k, SHARDS)
        slot, length = jnp.int32(0), jnp.int32(0)
        for i in range(STEPS):
            here = dest_shard[i] == shard
            slot = jnp.maximum(slot, jnp.where(here, i, 0))
            length = jnp.maximum(length, jnp.where(here, lengths[i], 0))
        slot_of.append(slot)
        tile = jnp.zeros((8, 128), jnp.int32) + length
        if k == BEFORE:
            sizes[k] = tile
        else:
            sizes_out[k] = tile

    def size_copy(k):
        return pltpu.make_async_remote_copy(
            src_ref=sizes_out.at[k],
            dst_ref=sizes.at[k],
            send_sem=size_send.at[k],
            recv_sem=size_recv.at[k],
            device_id=along_dp(k - BEFORE),
            device_id_type=MESH,
        )

    def send_copy(chunk, k):
        return pltpu.make_async_remote_copy(
            src_ref=outbox.at[chunk, k],
            dst_ref=inbox.at[chunk, pl.ds(k * SLOT, SLOT)],
            send_sem=send_sem.at[chunk, k],
            recv_sem=recv_sem.at[chunk, k],
            device_id=along_dp(k - BEFORE),
            device_id_type=MESH,
        )

    others = [k for k in range(STEPS) if k != BEFORE]

    def order_slots(chunk, load):
        for k in range(STEPS):
            if k == BEFORE:
                inbox[chunk, k * SLOT : (k + 1) * SLOT, :] = load(slot_of[k])
            else:
                outbox[chunk, k] = load(slot_of[k])

    slot_copy(0).wait()
    order_slots(0, lambda slot: first_slots[slot])

    pl.semaphore_wait(barrier, len(peers))

    for k in others:
        size_copy(k).start()
    for k in others:
        send_copy(0, k).start()
    for chunk in range(1, CHUNKS):
        slot_copy(chunk).wait()

    def send_chunk(chunk, carry):
        order_slots(chunk, lambda slot: slots[chunk - 1, slot])
        for k in others:
            send_copy(chunk, k).start()
        return carry

    lax.fori_loop(1, CHUNKS, send_chunk, 0)

    total[...] = jnp.zeros_like(total)
    squares[...] = jnp.zeros_like(squares)
    head_terms[...] = jnp.zeros_like(head_terms)
    key_rot[0:SLOT, :] = jnp.zeros((SLOT, HD), BF16)
    value_rows[0:SLOT, :] = jnp.zeros((SLOT, HD), BF16)

    for k in others:
        size_copy(k).wait_recv()
    size = [sizes[k, 0:1, :] for k in range(STEPS)]
    offset = [jnp.zeros_like(size[0])]
    for k in range(1, STEPS):
        offset.append(offset[-1] + size[k - 1])

    def step_start(row):
        start = jnp.zeros_like(row)
        for k in range(1, STEPS):
            start = jnp.where(row >= offset[k], offset[k], start)
        return start

    packed_row = lax.broadcasted_iota(jnp.int32, (PACK, 128), 0)
    for block in range(STEPS * SLOT // 128):
        column = lax.broadcasted_iota(jnp.int32, (1, 128), 1) + block * 128
        target = jnp.zeros_like(column)
        for k in range(block * 128 // SLOT, (block * 128 + 127) // SLOT + 1):
            position = column - k * SLOT
            row = jnp.where(position < size[k], offset[k] + position, -1)
            target = jnp.where(position >= 0, row, target)
        select[:, block * 128 : (block + 1) * 128] = jnp.where(packed_row == target, 1.0, 0.0).astype(BF16)

    def ring_copy(way, chunk):
        return pltpu.make_async_remote_copy(
            src_ref=rows.at[0, chunk],
            dst_ref=rows.at[1 + way, chunk],
            send_sem=ring_send.at[way, chunk],
            recv_sem=ring_recv.at[way, chunk],
            device_id=along_mp(1 - 2 * way),
            device_id_type=MESH,
        )

    def pass_copy(way, chunk):
        half = pl.ds(way * HALF, HALF)
        return pltpu.make_async_remote_copy(
            src_ref=rows.at[1 + way, chunk, half],
            dst_ref=rows.at[3, chunk, half],
            send_sem=pass_send.at[way, chunk],
            recv_sem=pass_recv.at[way, chunk],
            device_id=along_mp(1 - 2 * way),
            device_id_type=MESH,
        )

    def pack(chunk):
        for k in others:
            send_copy(chunk, k).wait_recv()
        packed = jnp.dot(select[...], inbox[chunk], preferred_element_type=F32)
        rows[0, chunk] = packed.astype(BF16)

    def head_term(chunk):
        parts = thirds(wide_row(value_head, chunk))
        sub = lax.broadcasted_iota(jnp.int32, (8, WIDTH), 0)
        stacked = jnp.zeros((8, WIDTH), F32)
        for i, part in enumerate(parts):
            stacked = jnp.where(sub == i, part.astype(F32), stacked)
        head_terms[...] += dot_last(stacked.astype(BF16), rows[0, chunk])

    def project(source, plane, chunk):
        block = plane * CHUNKS + chunk
        x = rows[source, chunk].astype(F32)
        squared = x * x
        squares[...] += squared[:, :128] + squared[:, 128:]
        scaled = (x * wide_row(gain, block)).astype(BF16)
        for n in range(COLS // WIDTH):
            columns = slice(n * WIDTH, (n + 1) * WIDTH)
            total[:, columns] += jnp.dot(
                scaled, weights[block, :, columns], preferred_element_type=F32
            )

    def ring_start(chunk):
        for way in range(2):
            ring_copy(way, chunk).start()

    pack(0)
    ring_start(0)

    half_sign = jnp.where(lax.broadcasted_iota(jnp.int32, (TILE, TILE), 1) < HD // 2, -1.0, 1.0)
    for b in range(TILES):
        at = slice(b * TILE, (b + 1) * TILE)
        row = lax.broadcasted_iota(jnp.int32, (TILE, TILE), 0) + b * TILE
        angle = (row - step_start(row)).astype(F32) * frequency[...]
        cosines[at, :] = jnp.cos(angle)
        sines[at, :] = jnp.sin(angle) * half_sign

    for copy in weight_copies:
        copy.wait()

    def advance(t, carry):
        @pl.when(t + 1 < CHUNKS)
        def _():
            pack(t + 1)
            ring_start(t + 1)

        @pl.when(t < CHUNKS)
        def _():
            head_term(t)
            project(0, mp, t)
            for way in range(2):
                ring_copy(way, t).wait_recv()
                pass_copy(way, t).start()

            def near(source, inner):
                project(source, lax.rem(mp + 2 * source - 3 + PLANES, PLANES), t)
                return inner

            lax.fori_loop(1, 3, near, 0)

        @pl.when(t >= 1)
        def _():
            for way in range(2):
                pass_copy(way, t - 1).wait_recv()
            project(3, lax.rem(mp + 2, PLANES), t - 1)

        return carry

    lax.fori_loop(0, CHUNKS + 1, advance, 0)

    query_scale = math.log2(math.e) / math.sqrt(HD)

    def rotate(b):
        at = slice(b * TILE, (b + 1) * TILE)
        below = slice(SLOT + b * TILE, SLOT + (b + 1) * TILE)
        mean = jnp.sum(squares[at, :], axis=1, keepdims=True) / (PLANES * CHUNKS * WIDTH)
        scale = lax.rsqrt(mean + EPSILON)
        cosine, sine = cosines[at, :], sines[at, :]

        def turned(head):
            x = total[at, head * HD : (head + 1) * HD] * scale
            return x * cosine + pltpu.roll(x, HD // 2, 1) * sine

        for head in range(HEADS):
            query_rot[b, head * TILE : (head + 1) * TILE, :] = (turned(head) * query_scale).astype(BF16)
        key_rot[below, :] = turned(HEADS).astype(BF16)
        value_rows[below, :] = (total[at, (HEADS + 1) * HD :] * scale).astype(BF16)

    folded = jnp.concatenate([part.astype(F32) for part in thirds(folded_head[...])], axis=0).astype(BF16)
    reach = lax.broadcasted_iota(jnp.int32, (BAND, TILE), 0) - SLOT
    query_at = lax.broadcasted_iota(jnp.int32, (BAND, TILE), 1)
    lane = lax.broadcasted_iota(jnp.int32, (1, TILE), 1)
    step_sub = lax.broadcasted_iota(jnp.int32, (STEPS, TILE), 0)
    time_sub = lax.broadcasted_iota(jnp.int32, (LANES, TILE), 0)

    def attend(b):
        band = slice(b * TILE, b * TILE + BAND)
        keys = key_rot[band, :]
        row = lane + b * TILE
        start = step_start(row)
        step_row = jnp.zeros_like(row)
        for k in range(1, STEPS):
            step_row = step_row + jnp.where(row >= offset[k], 1, 0)
        position_row = row - start
        allowed = (reach <= query_at) & (reach >= start - b * TILE)
        through = sum_of_thirds(dot_last(folded, value_rows[band, :]))
        high, low, _ = thirds(through)
        lifted = jnp.concatenate(
            [high.astype(F32), low.astype(F32), jnp.ones((HEADS, BAND), F32)], axis=0
        ).astype(BF16)
        head_weights = []
        for head in range(HEADS):
            scores = dot_last(keys, query_rot[b, head * TILE : (head + 1) * TILE, :])
            scores = jnp.where(allowed, scores, -1e30)
            peak = jnp.max(scores, axis=0, keepdims=True)
            head_weights.append(jnp.exp2(scores - peak).astype(BF16))
        sums = jnp.dot(lifted, jnp.concatenate(head_weights, axis=1), preferred_element_type=F32)
        ends = head_terms[:, b * TILE : (b + 1) * TILE]
        term = ends[0:1] + ends[1:2] + ends[2:3]
        for head in range(HEADS):
            part = slice(head * TILE, (head + 1) * TILE)
            above = sums[head : head + 1, part] + sums[HEADS + head : HEADS + head + 1, part]
            term = term + above / sums[2 * HEADS : 2 * HEADS + 1, part]
        spread = jnp.where(step_sub == step_row, term, 0.0)
        spread = jnp.concatenate([part.astype(F32) for part in thirds(spread)], axis=0).astype(BF16)
        placed = jnp.where(time_sub == position_row, 1.0, 0.0).astype(BF16)
        return sum_of_thirds(dot_last(spread, placed))

    for b in range(TILES):
        rotate(b)
    shares = attend(0)
    for b in range(1, TILES):
        shares = shares + attend(b)

    def back_copy(k):
        return pltpu.make_async_remote_copy(
            src_ref=by_step.at[k],
            dst_ref=arrived.at[k],
            send_sem=back_send.at[k],
            recv_sem=back_recv.at[k],
            device_id=along_dp(BEFORE - k),
            device_id_type=MESH,
        )

    for k in range(STEPS):
        one = jnp.broadcast_to(shares[k : k + 1, :], (8, LANES))
        if k == BEFORE:
            arrived[k] = one
        else:
            by_step[k] = one
    for k in others:
        back_copy(k).start()
    padded_rewards[...] = jnp.zeros_like(padded_rewards)
    padded_rewards[:, 0:SLOT] = rewards[...]
    for k in others:
        back_copy(k).wait_recv()

    sub = lax.broadcasted_iota(jnp.int32, (STEPS, LANES), 0)
    time = lax.broadcasted_iota(jnp.int32, (STEPS, LANES), 1)
    slot_share = jnp.zeros((STEPS, LANES), F32)
    length = jnp.zeros((STEPS, LANES), jnp.int32)
    for i in range(STEPS):
        step = jnp.minimum(lax.rem(dest_shard[i] - dp + SHARDS, SHARDS), STEPS - 1)
        slot_share = jnp.where(sub == i, arrived[step], slot_share)
        length = jnp.where(sub == i, lengths[i], length)

    by_plane[mp] = slot_share

    def plane_copy(by, plane):
        return pltpu.make_async_remote_copy(
            src_ref=by_plane.at[plane],
            dst_ref=by_plane.at[plane],
            send_sem=plane_send.at[by - 1],
            recv_sem=plane_recv.at[by - 1],
            device_id=along_mp(by),
            device_id_type=MESH,
        )

    for by in range(1, PLANES):
        plane_copy(by, mp).start()
    for by in range(1, PLANES):
        plane_copy(by, along_mp(-by)[1]).wait_recv()
    slot_values = (by_plane[0] + by_plane[1]) + (by_plane[2] + by_plane[3])
    live = time < length
    values = jnp.where(live, slot_values, 0.0)
    following = jnp.where(time + 1 < length, pltpu.roll(values, LANES - 1, 1), 0.0)
    advantages = jnp.where(live, padded_rewards[...] + DISCOUNT * following - values, 0.0)
    shift = 1
    while shift < SLOT:
        later = jnp.where(time < LANES - shift, pltpu.roll(advantages, LANES - shift, 1), 0.0)
        advantages = advantages + (DISCOUNT * SMOOTHING) ** shift * later
        shift *= 2
    both_out[0:STEPS, :] = values
    both_out[STEPS:, :] = advantages

    for k in others:
        size_copy(k).wait_send()

    def drain(chunk, carry):
        for k in others:
            send_copy(chunk, k).wait_send()
        for way in range(2):
            ring_copy(way, chunk).wait_send()
            pass_copy(way, chunk).wait_send()
        return carry

    lax.fori_loop(0, CHUNKS, drain, 0)
    for by in range(1, PLANES):
        plane_copy(by, mp).wait_send()
    for k in others:
        back_copy(k).wait_send()


def local(
    hidden,
    rewards,
    lengths,
    dest_shard,
    source_owner,
    pack_offset,
    segment_ids,
    norm_gain,
    w_query,
    w_key,
    w_value,
    value_head,
    folded_head,
):
    blocks = PLANES * CHUNKS
    half = HD // 2
    frequency = (ROPE_BASE ** (-np.arange(half, dtype=np.float64) / half)).astype(np.float32)
    frequency = jnp.asarray(np.concatenate([frequency, frequency])[None, :])
    smem = pl.BlockSpec(memory_space=pltpu.SMEM)
    vmem = pl.BlockSpec(memory_space=pltpu.VMEM)
    hbm = pl.BlockSpec(memory_space=pl.ANY)
    dma = pltpu.SemaphoreType.DMA
    both = pl.pallas_call(
        kernel,
        name="critic",
        out_shape=jax.ShapeDtypeStruct((2 * STEPS, LANES), F32),
        in_specs=[smem] * 2 + [vmem] * 5 + [hbm] * 4,
        out_specs=vmem,
        scratch_shapes=[
            pltpu.VMEM((STEPS, SLOT, WIDTH), BF16),
            pltpu.VMEM((CHUNKS - 1, STEPS, SLOT, WIDTH), BF16),
            pltpu.VMEM((CHUNKS, STEPS, SLOT, WIDTH), BF16),
            pltpu.VMEM((CHUNKS, STEPS * SLOT, WIDTH), BF16),
            pltpu.VMEM((blocks, WIDTH, COLS), BF16),
            pltpu.VMEM((PLANES, CHUNKS, PACK, WIDTH), BF16),
            pltpu.VMEM((PACK, COLS), F32),
            pltpu.VMEM((PACK, 128), F32),
            pltpu.VMEM((8, PACK), F32),
            pltpu.VMEM((PACK, STEPS * SLOT), BF16),
            pltpu.VMEM((PACK, HD), F32),
            pltpu.VMEM((PACK, HD), F32),
            pltpu.VMEM((STEPS, 8, 128), jnp.int32),
            pltpu.VMEM((STEPS, 8, 128), jnp.int32),
            pltpu.VMEM((TILES, HEADS * TILE, HD), BF16),
            pltpu.VMEM((SLOT + PACK, HD), BF16),
            pltpu.VMEM((SLOT + PACK, HD), BF16),
            pltpu.VMEM((PLANES, STEPS, LANES), F32),
            pltpu.VMEM((STEPS, 8, LANES), F32),
            pltpu.VMEM((STEPS, 8, LANES), F32),
            pltpu.VMEM((STEPS, LANES), F32),
            dma((CHUNKS,)),
            dma((3,)),
            dma((STEPS,)),
            dma((STEPS,)),
            dma((CHUNKS, STEPS)),
            dma((CHUNKS, STEPS)),
            dma((2, CHUNKS)),
            dma((2, CHUNKS)),
            dma((2, CHUNKS)),
            dma((2, CHUNKS)),
            dma((3,)),
            dma((3,)),
            dma((STEPS,)),
            dma((STEPS,)),
        ],
        compiler_params=pltpu.CompilerParams(
            collective_id=0, has_side_effects=True, vmem_limit_bytes=67_043_328
        ),
    )(
        lengths,
        dest_shard,
        norm_gain.reshape(2 * blocks, 128),
        value_head.reshape(2 * CHUNKS, 128),
        folded_head.reshape(HEADS, HD),
        frequency,
        rewards,
        hidden.reshape(STEPS, SLOT, CHUNKS * WIDTH),
        w_query.reshape(blocks, WIDTH, HEADS * HD),
        w_key.reshape(blocks, WIDTH, HD),
        w_value.reshape(blocks, WIDTH, HD),
    )
    return both[:STEPS, :SLOT], both[STEPS:, :SLOT]


def solution(mesh):
    return jax.shard_map(
        local,
        mesh=mesh,
        in_specs=(
            P("dp", "mp"),
            P("dp", None),
            P("dp"),
            P("dp"),
            P("dp"),
            P("dp"),
            P("dp"),
            P(),
            P(None, "mp"),
            P(None, "mp"),
            P(None, "mp"),
            P("mp"),
            P("mp"),
        ),
        out_specs=(P("dp", None), P("dp", None)),
        check_vma=False,
    )
```

```python
import math

import jax
import jax.numpy as jnp
import numpy as np
from jax import lax
from jax.experimental import pallas as pl
from jax.experimental.pallas import tpu as pltpu
from jax.sharding import PartitionSpec as P

MESH = pl.DeviceIdType.MESH
F32 = jnp.float32
BF16 = jnp.bfloat16

HD = 128
EPSILON = 1e-05
DISCOUNT = 0.99
SMOOTHING = 0.95
ROPE_BASE = 500000.0

SHARDS = 32
PLANES = 4
STEPS = 8
SLOT = 160
PACK = 640
TILE = 128
TILES = PACK // TILE
WIDTH = 256
CHUNKS = 8
HEADS = 8
COLS = HEADS * HD + 2 * HD
BAND = SLOT + TILE
LANES = 256
BEFORE = 4
HALF = PACK // 2


CONTRACT_LAST = (((1,), (1,)), ((), ()))


def dot_last(a, b):
    return lax.dot_general(a, b, CONTRACT_LAST, preferred_element_type=F32)


def thirds(value):
    high = value.astype(BF16)
    rest = value - high.astype(F32)
    middle = rest.astype(BF16)
    return high, middle, (rest - middle.astype(F32)).astype(BF16)


def wide_row(ref, row):
    return jnp.concatenate([ref[pl.ds(2 * row + i, 1), :] for i in range(2)], axis=1)


def sum_of_thirds(stacked):
    rows = stacked.shape[0] // 3
    return stacked[:rows] + stacked[rows : 2 * rows] + stacked[2 * rows :]


def kernel(
    lengths,
    dest_shard,
    gain_in,
    value_head_in,
    folded_head_in,
    frequency_in,
    rewards_in,
    hidden,
    w_query,
    w_key,
    w_value,
    both_out,
    gain,
    value_head,
    folded_head,
    frequency,
    rewards,
    first_slots,
    slots,
    outbox,
    inbox,
    weights,
    rows,
    total,
    squares,
    head_terms,
    select,
    cosines,
    sines,
    sizes_out,
    sizes,
    query_rot,
    key_rot,
    value_rows,
    by_step,
    arrived,
    padded_rewards,
    small_sem,
    slot_sem,
    weight_sem,
    size_send,
    size_recv,
    send_sem,
    recv_sem,
    ring_send,
    ring_recv,
    pass_send,
    pass_recv,
    back_send,
    back_recv,
):
    dp = lax.axis_index("dp")
    mp = lax.axis_index("mp")

    def along_dp(by):
        return lax.rem(dp + (by + SHARDS), SHARDS), mp

    def along_mp(by):
        return dp, lax.rem(mp + (by + PLANES), PLANES)

    barrier = pltpu.get_barrier_semaphore()
    peers = [along_dp(by) for by in range(-BEFORE, BEFORE + 1) if by]
    peers += [along_mp(by) for by in (1, -1, 2)]
    for peer in peers:
        pl.semaphore_signal(barrier, inc=1, device_id=peer, device_id_type=MESH)

    def slot_copy(chunk):
        columns = pl.ds(chunk * WIDTH, WIDTH)
        target = first_slots if chunk == 0 else slots.at[chunk - 1]
        return pltpu.make_async_copy(hidden.at[:, :, columns], target, slot_sem.at[chunk])

    weight_copies = [
        pltpu.make_async_copy(source, weights.at[:, :, pl.ds(start, source.shape[2])], weight_sem.at[i])
        for i, (source, start) in enumerate(
            ((w_query, 0), (w_key, HEADS * HD), (w_value, HEADS * HD + HD))
        )
    ]
    small_copies = [
        pltpu.make_async_copy(source, target, small_sem.at[i])
        for i, (source, target) in enumerate(
            (
                (gain_in, gain),
                (value_head_in, value_head),
                (folded_head_in, folded_head),
                (frequency_in, frequency),
                (rewards_in, rewards),
            )
        )
    ]
    for chunk in range(CHUNKS):
        slot_copy(chunk).start()
    for copy in small_copies:
        copy.start()
    for copy in weight_copies:
        copy.start()

    slot_of = []
    for k in range(STEPS):
        shard = lax.rem(dp + k, SHARDS)
        slot, length = jnp.int32(0), jnp.int32(0)
        for i in range(STEPS):
            here = dest_shard[i] == shard
            slot = jnp.maximum(slot, jnp.where(here, i, 0))
            length = jnp.maximum(length, jnp.where(here, lengths[i], 0))
        slot_of.append(slot)
        tile = jnp.zeros((8, 128), jnp.int32) + length
        if k == BEFORE:
            sizes[k] = tile
        else:
            sizes_out[k] = tile

    def size_copy(k):
        return pltpu.make_async_remote_copy(
            src_ref=sizes_out.at[k],
            dst_ref=sizes.at[k],
            send_sem=size_send.at[k],
            recv_sem=size_recv.at[k],
            device_id=along_dp(k - BEFORE),
            device_id_type=MESH,
        )

    def send_copy(chunk, k):
        return pltpu.make_async_remote_copy(
            src_ref=outbox.at[chunk, k],
            dst_ref=inbox.at[chunk, pl.ds(k * SLOT, SLOT)],
            send_sem=send_sem.at[chunk, k],
            recv_sem=recv_sem.at[chunk, k],
            device_id=along_dp(k - BEFORE),
            device_id_type=MESH,
        )

    others = [k for k in range(STEPS) if k != BEFORE]

    def order_slots(chunk, load):
        for k in range(STEPS):
            if k == BEFORE:
                inbox[chunk, k * SLOT : (k + 1) * SLOT, :] = load(slot_of[k])
            else:
                outbox[chunk, k] = load(slot_of[k])

    slot_copy(0).wait()
    order_slots(0, lambda slot: first_slots[slot])

    pl.semaphore_wait(barrier, len(peers))

    for k in others:
        size_copy(k).start()
    for k in others:
        send_copy(0, k).start()
    for chunk in range(1, CHUNKS):
        slot_copy(chunk).wait()

    def send_chunk(chunk, carry):
        order_slots(chunk, lambda slot: slots[chunk - 1, slot])
        for k in others:
            send_copy(chunk, k).start()
        return carry

    lax.fori_loop(1, CHUNKS, send_chunk, 0)

    total[...] = jnp.zeros_like(total)
    squares[...] = jnp.zeros_like(squares)
    head_terms[...] = jnp.zeros_like(head_terms)
    key_rot[0:SLOT, :] = jnp.zeros((SLOT, HD), BF16)
    value_rows[0:SLOT, :] = jnp.zeros((SLOT, HD), BF16)

    for k in others:
        size_copy(k).wait_recv()
    size = [sizes[k, 0:1, :] for k in range(STEPS)]
    offset = [jnp.zeros_like(size[0])]
    for k in range(1, STEPS):
        offset.append(offset[-1] + size[k - 1])

    def step_start(row):
        start = jnp.zeros_like(row)
        for k in range(1, STEPS):
            start = jnp.where(row >= offset[k], offset[k], start)
        return start

    packed_row = lax.broadcasted_iota(jnp.int32, (PACK, 128), 0)
    for block in range(STEPS * SLOT // 128):
        column = lax.broadcasted_iota(jnp.int32, (1, 128), 1) + block * 128
        target = jnp.zeros_like(column)
        for k in range(block * 128 // SLOT, (block * 128 + 127) // SLOT + 1):
            position = column - k * SLOT
            row = jnp.where(position < size[k], offset[k] + position, -1)
            target = jnp.where(position >= 0, row, target)
        select[:, block * 128 : (block + 1) * 128] = jnp.where(packed_row == target, 1.0, 0.0).astype(BF16)

    def ring_copy(way, chunk):
        return pltpu.make_async_remote_copy(
            src_ref=rows.at[0, chunk],
            dst_ref=rows.at[1 + way, chunk],
            send_sem=ring_send.at[way, chunk],
            recv_sem=ring_recv.at[way, chunk],
            device_id=along_mp(1 - 2 * way),
            device_id_type=MESH,
        )

    def pass_copy(way, chunk):
        half = pl.ds(way * HALF, HALF)
        return pltpu.make_async_remote_copy(
            src_ref=rows.at[1 + way, chunk, half],
            dst_ref=rows.at[3, chunk, half],
            send_sem=pass_send.at[way, chunk],
            recv_sem=pass_recv.at[way, chunk],
            device_id=along_mp(1 - 2 * way),
            device_id_type=MESH,
        )

    def pack(chunk):
        for k in others:
            send_copy(chunk, k).wait_recv()
        packed = jnp.dot(select[...], inbox[chunk], preferred_element_type=F32)
        rows[0, chunk] = packed.astype(BF16)

    def head_term(chunk):
        parts = thirds(wide_row(value_head, chunk))
        sub = lax.broadcasted_iota(jnp.int32, (8, WIDTH), 0)
        stacked = jnp.zeros((8, WIDTH), F32)
        for i, part in enumerate(parts):
            stacked = jnp.where(sub == i, part.astype(F32), stacked)
        head_terms[...] += dot_last(stacked.astype(BF16), rows[0, chunk])

    def project(source, plane, chunk):
        block = plane * CHUNKS + chunk
        x = rows[source, chunk].astype(F32)
        squared = x * x
        squares[...] += squared[:, :128] + squared[:, 128:]
        scaled = (x * wide_row(gain, block)).astype(BF16)
        for n in range(COLS // WIDTH):
            columns = slice(n * WIDTH, (n + 1) * WIDTH)
            total[:, columns] += jnp.dot(
                scaled, weights[block, :, columns], preferred_element_type=F32
            )

    def ring_start(chunk):
        for way in range(2):
            ring_copy(way, chunk).start()

    pack(0)
    ring_start(0)

    for copy in small_copies:
        copy.wait()

    half_sign = jnp.where(lax.broadcasted_iota(jnp.int32, (TILE, TILE), 1) < HD // 2, -1.0, 1.0)
    for b in range(TILES):
        at = slice(b * TILE, (b + 1) * TILE)
        row = lax.broadcasted_iota(jnp.int32, (TILE, TILE), 0) + b * TILE
        angle = (row - step_start(row)).astype(F32) * frequency[...]
        cosines[at, :] = jnp.cos(angle)
        sines[at, :] = jnp.sin(angle) * half_sign

    for copy in weight_copies:
        copy.wait()

    def advance(t, carry):
        @pl.when(t + 1 < CHUNKS)
        def _():
            pack(t + 1)
            ring_start(t + 1)

        @pl.when(t < CHUNKS)
        def _():
            head_term(t)
            project(0, mp, t)
            for way in range(2):
                ring_copy(way, t).wait_recv()
                pass_copy(way, t).start()

            def near(source, inner):
                project(source, lax.rem(mp + 2 * source - 3 + PLANES, PLANES), t)
                return inner

            lax.fori_loop(1, 3, near, 0)

        @pl.when(t >= 1)
        def _():
            for way in range(2):
                pass_copy(way, t - 1).wait_recv()
            project(3, lax.rem(mp + 2, PLANES), t - 1)

        return carry

    lax.fori_loop(0, CHUNKS + 1, advance, 0)

    query_scale = math.log2(math.e) / math.sqrt(HD)

    def rotate(b):
        at = slice(b * TILE, (b + 1) * TILE)
        below = slice(SLOT + b * TILE, SLOT + (b + 1) * TILE)
        mean = jnp.sum(squares[at, :], axis=1, keepdims=True) / (PLANES * CHUNKS * WIDTH)
        scale = lax.rsqrt(mean + EPSILON)
        cosine, sine = cosines[at, :], sines[at, :]

        def turned(head):
            x = total[at, head * HD : (head + 1) * HD] * scale
            return x * cosine + pltpu.roll(x, HD // 2, 1) * sine

        for head in range(HEADS):
            query_rot[b, head * TILE : (head + 1) * TILE, :] = (turned(head) * query_scale).astype(BF16)
        key_rot[below, :] = turned(HEADS).astype(BF16)
        value_rows[below, :] = (total[at, (HEADS + 1) * HD :] * scale).astype(BF16)

    folded = jnp.concatenate([part.astype(F32) for part in thirds(folded_head[...])], axis=0).astype(BF16)
    reach = lax.broadcasted_iota(jnp.int32, (BAND, TILE), 0) - SLOT
    query_at = lax.broadcasted_iota(jnp.int32, (BAND, TILE), 1)
    lane = lax.broadcasted_iota(jnp.int32, (1, TILE), 1)
    step_sub = lax.broadcasted_iota(jnp.int32, (STEPS, TILE), 0)
    time_sub = lax.broadcasted_iota(jnp.int32, (LANES, TILE), 0)

    def attend(b):
        band = slice(b * TILE, b * TILE + BAND)
        keys = key_rot[band, :]
        row = lane + b * TILE
        start = step_start(row)
        step_row = jnp.zeros_like(row)
        for k in range(1, STEPS):
            step_row = step_row + jnp.where(row >= offset[k], 1, 0)
        position_row = row - start
        allowed = (reach <= query_at) & (reach >= start - b * TILE)
        through = sum_of_thirds(dot_last(folded, value_rows[band, :]))
        high, low, _ = thirds(through)
        lifted = jnp.concatenate(
            [high.astype(F32), low.astype(F32), jnp.ones((HEADS, BAND), F32)], axis=0
        ).astype(BF16)
        head_weights = []
        for head in range(HEADS):
            scores = dot_last(keys, query_rot[b, head * TILE : (head + 1) * TILE, :])
            scores = jnp.where(allowed, scores, -1e30)
            peak = jnp.max(scores, axis=0, keepdims=True)
            head_weights.append(jnp.exp2(scores - peak).astype(BF16))
        sums = jnp.dot(lifted, jnp.concatenate(head_weights, axis=1), preferred_element_type=F32)
        ends = head_terms[:, b * TILE : (b + 1) * TILE]
        term = ends[0:1] + ends[1:2] + ends[2:3]
        for head in range(HEADS):
            part = slice(head * TILE, (head + 1) * TILE)
            above = sums[head : head + 1, part] + sums[HEADS + head : HEADS + head + 1, part]
            term = term + above / sums[2 * HEADS : 2 * HEADS + 1, part]
        spread = jnp.where(step_sub == step_row, term, 0.0)
        spread = jnp.concatenate([part.astype(F32) for part in thirds(spread)], axis=0).astype(BF16)
        placed = jnp.where(time_sub == position_row, 1.0, 0.0).astype(BF16)
        return sum_of_thirds(dot_last(spread, placed))

    for b in range(TILES):
        rotate(b)
    shares = attend(0)
    for b in range(1, TILES):
        shares = shares + attend(b)

    def back_copy(by, k, plane):
        return pltpu.make_async_remote_copy(
            src_ref=by_step.at[k],
            dst_ref=arrived.at[plane, k],
            send_sem=back_send.at[by, k],
            recv_sem=back_recv.at[by, k],
            device_id=(along_dp(BEFORE - k)[0], along_mp(by)[1]),
            device_id_type=MESH,
        )

    remote = [(by, k) for k in range(STEPS) for by in range(PLANES) if by or k != BEFORE]
    for k in range(STEPS):
        for half in range(LANES // 128):
            by_step[k, half : half + 1, :] = shares[k : k + 1, half * 128 : (half + 1) * 128]
    for by, k in remote:
        back_copy(by, k, mp).start()
    arrived[mp, BEFORE] = by_step[BEFORE]
    padded_rewards[...] = jnp.zeros_like(padded_rewards)
    padded_rewards[:, 0:SLOT] = rewards[...]
    for by, k in remote:
        back_copy(by, k, along_mp(-by)[1]).wait_recv()

    sub = lax.broadcasted_iota(jnp.int32, (STEPS, LANES), 0)
    time = lax.broadcasted_iota(jnp.int32, (STEPS, LANES), 1)
    slot_values = jnp.zeros((STEPS, LANES), F32)
    length = jnp.zeros((STEPS, LANES), jnp.int32)
    for i in range(STEPS):
        step = jnp.minimum(lax.rem(dest_shard[i] - dp + SHARDS, SHARDS), STEPS - 1)
        both = (arrived[0, step] + arrived[1, step]) + (arrived[2, step] + arrived[3, step])
        line = jnp.concatenate([both[0:1], both[1:2]], axis=1)
        slot_values = jnp.where(sub == i, line, slot_values)
        length = jnp.where(sub == i, lengths[i], length)
    live = time < length
    values = jnp.where(live, slot_values, 0.0)
    following = jnp.where(time + 1 < length, pltpu.roll(values, LANES - 1, 1), 0.0)
    advantages = jnp.where(live, padded_rewards[...] + DISCOUNT * following - values, 0.0)
    shift = 1
    while shift < SLOT:
        later = jnp.where(time < LANES - shift, pltpu.roll(advantages, LANES - shift, 1), 0.0)
        advantages = advantages + (DISCOUNT * SMOOTHING) ** shift * later
        shift *= 2
    both_out[0:STEPS, :] = values
    both_out[STEPS:, :] = advantages

    for k in others:
        size_copy(k).wait_send()

    def drain(chunk, carry):
        for k in others:
            send_copy(chunk, k).wait_send()
        for way in range(2):
            ring_copy(way, chunk).wait_send()
            pass_copy(way, chunk).wait_send()
        return carry

    lax.fori_loop(0, CHUNKS, drain, 0)
    for by, k in remote:
        back_copy(by, k, mp).wait_send()


def local(
    hidden,
    rewards,
    lengths,
    dest_shard,
    source_owner,
    pack_offset,
    segment_ids,
    norm_gain,
    w_query,
    w_key,
    w_value,
    value_head,
    folded_head,
):
    blocks = PLANES * CHUNKS
    half = HD // 2
    frequency = (ROPE_BASE ** (-np.arange(half, dtype=np.float64) / half)).astype(np.float32)
    frequency = jnp.asarray(np.concatenate([frequency, frequency])[None, :])
    smem = pl.BlockSpec(memory_space=pltpu.SMEM)
    vmem = pl.BlockSpec(memory_space=pltpu.VMEM)
    hbm = pl.BlockSpec(memory_space=pl.ANY)
    dma = pltpu.SemaphoreType.DMA
    both = pl.pallas_call(
        kernel,
        name="critic",
        out_shape=jax.ShapeDtypeStruct((2 * STEPS, LANES), F32),
        in_specs=[smem] * 2 + [hbm] * 9,
        out_specs=vmem,
        scratch_shapes=[
            pltpu.VMEM((2 * blocks, 128), F32),
            pltpu.VMEM((2 * CHUNKS, 128), F32),
            pltpu.VMEM((HEADS, HD), F32),
            pltpu.VMEM((1, HD), F32),
            pltpu.VMEM((STEPS, SLOT), F32),
            pltpu.VMEM((STEPS, SLOT, WIDTH), BF16),
            pltpu.VMEM((CHUNKS - 1, STEPS, SLOT, WIDTH), BF16),
            pltpu.VMEM((CHUNKS, STEPS, SLOT, WIDTH), BF16),
            pltpu.VMEM((CHUNKS, STEPS * SLOT, WIDTH), BF16),
            pltpu.VMEM((blocks, WIDTH, COLS), BF16),
            pltpu.VMEM((PLANES, CHUNKS, PACK, WIDTH), BF16),
            pltpu.VMEM((PACK, COLS), F32),
            pltpu.VMEM((PACK, 128), F32),
            pltpu.VMEM((8, PACK), F32),
            pltpu.VMEM((PACK, STEPS * SLOT), BF16),
            pltpu.VMEM((PACK, HD), F32),
            pltpu.VMEM((PACK, HD), F32),
            pltpu.VMEM((STEPS, 8, 128), jnp.int32),
            pltpu.VMEM((STEPS, 8, 128), jnp.int32),
            pltpu.VMEM((TILES, HEADS * TILE, HD), BF16),
            pltpu.VMEM((SLOT + PACK, HD), BF16),
            pltpu.VMEM((SLOT + PACK, HD), BF16),
            pltpu.VMEM((STEPS, LANES // 128, 128), F32),
            pltpu.VMEM((PLANES, STEPS, LANES // 128, 128), F32),
            pltpu.VMEM((STEPS, LANES), F32),
            dma((5,)),
            dma((CHUNKS,)),
            dma((3,)),
            dma((STEPS,)),
            dma((STEPS,)),
            dma((CHUNKS, STEPS)),
            dma((CHUNKS, STEPS)),
            dma((2, CHUNKS)),
            dma((2, CHUNKS)),
            dma((2, CHUNKS)),
            dma((2, CHUNKS)),
            dma((PLANES, STEPS)),
            dma((PLANES, STEPS)),
        ],
        compiler_params=pltpu.CompilerParams(
            collective_id=0, has_side_effects=True, vmem_limit_bytes=67_043_328
        ),
    )(
        lengths,
        dest_shard,
        norm_gain.reshape(2 * blocks, 128),
        value_head.reshape(2 * CHUNKS, 128),
        folded_head.reshape(HEADS, HD),
        frequency,
        rewards,
        hidden.reshape(STEPS, SLOT, CHUNKS * WIDTH),
        w_query.reshape(blocks, WIDTH, HEADS * HD),
        w_key.reshape(blocks, WIDTH, HD),
        w_value.reshape(blocks, WIDTH, HD),
    )
    return both[:STEPS, :SLOT], both[STEPS:, :SLOT]


def solution(mesh):
    return jax.shard_map(
        local,
        mesh=mesh,
        in_specs=(
            P("dp", "mp"),
            P("dp", None),
            P("dp"),
            P("dp"),
            P("dp"),
            P("dp"),
            P("dp"),
            P(),
            P(None, "mp"),
            P(None, "mp"),
            P(None, "mp"),
            P("mp"),
            P("mp"),
        ),
        out_specs=(P("dp", None), P("dp", None)),
        check_vma=False,
    )
```

```python
import math

import jax
import jax.numpy as jnp
import numpy as np
from jax import lax
from jax.experimental import pallas as pl
from jax.experimental.pallas import tpu as pltpu
from jax.sharding import PartitionSpec as P

MESH = pl.DeviceIdType.MESH
F32 = jnp.float32
BF16 = jnp.bfloat16

HD = 128
EPSILON = 1e-05
DISCOUNT = 0.99
SMOOTHING = 0.95
ROPE_BASE = 500000.0

SHARDS = 32
PLANES = 4
STEPS = 8
SLOT = 160
PACK = 640
TILE = 128
TILES = PACK // TILE
WIDTH = 256
CHUNKS = 8
HEADS = 8
COLS = HEADS * HD + 2 * HD
BAND = SLOT + TILE
LANES = 256
BEFORE = 4
HALF = PACK // 2
COLUMNS = (slice(0, WIDTH // 2), slice(WIDTH // 2, WIDTH))
SPLIT = 2


CONTRACT_LAST = (((1,), (1,)), ((), ()))


def dot_last(a, b):
    return lax.dot_general(a, b, CONTRACT_LAST, preferred_element_type=F32)


def thirds(value):
    high = value.astype(BF16)
    rest = value - high.astype(F32)
    middle = rest.astype(BF16)
    return high, middle, (rest - middle.astype(F32)).astype(BF16)


def wide_row(ref, row):
    return jnp.concatenate([ref[pl.ds(2 * row + i, 1), :] for i in range(2)], axis=1)


def sum_of_thirds(stacked):
    rows = stacked.shape[0] // 3
    return stacked[:rows] + stacked[rows : 2 * rows] + stacked[2 * rows :]


def kernel(
    lengths,
    dest_shard,
    gain_in,
    value_head_in,
    folded_head_in,
    frequency_in,
    rewards_in,
    hidden,
    w_query,
    w_key,
    w_value,
    both_out,
    gain,
    value_head,
    folded_head,
    frequency,
    rewards,
    first_slots,
    slots,
    outbox,
    inbox,
    weights,
    rows,
    total,
    squares,
    head_terms,
    select,
    cosines,
    sines,
    sizes_out,
    sizes,
    query_rot,
    key_rot,
    value_rows,
    by_step,
    arrived,
    padded_rewards,
    small_sem,
    slot_sem,
    weight_sem,
    size_send,
    size_recv,
    first_send,
    first_recv,
    early_send,
    early_recv,
    send_sem,
    recv_sem,
    ring_send,
    ring_recv,
    pass_send,
    pass_recv,
    back_send,
    back_recv,
):
    dp = lax.axis_index("dp")
    mp = lax.axis_index("mp")

    def along_dp(by):
        return lax.rem(dp + (by + SHARDS), SHARDS), mp

    def along_mp(by):
        return dp, lax.rem(mp + (by + PLANES), PLANES)

    barrier = pltpu.get_barrier_semaphore()
    peers = [along_dp(by) for by in range(-BEFORE, BEFORE + 1) if by]
    peers += [along_mp(by) for by in (1, -1, 2)]
    for peer in peers:
        pl.semaphore_signal(barrier, inc=1, device_id=peer, device_id_type=MESH)

    def slot_copy(chunk):
        columns = pl.ds(chunk * WIDTH, WIDTH)
        target = first_slots if chunk == 0 else slots.at[chunk - 1]
        return pltpu.make_async_copy(hidden.at[:, :, columns], target, slot_sem.at[chunk])

    weight_copies = [
        pltpu.make_async_copy(source, weights.at[:, :, pl.ds(start, source.shape[2])], weight_sem.at[i])
        for i, (source, start) in enumerate(
            ((w_query, 0), (w_key, HEADS * HD), (w_value, HEADS * HD + HD))
        )
    ]
    small_copies = [
        pltpu.make_async_copy(source, target, small_sem.at[i])
        for i, (source, target) in enumerate(
            (
                (gain_in, gain),
                (value_head_in, value_head),
                (folded_head_in, folded_head),
                (frequency_in, frequency),
                (rewards_in, rewards),
            )
        )
    ]
    for chunk in range(CHUNKS):
        slot_copy(chunk).start()
    for copy in small_copies:
        copy.start()
    for copy in weight_copies:
        copy.start()

    slot_of = []
    for k in range(STEPS):
        shard = lax.rem(dp + k, SHARDS)
        slot, length = jnp.int32(0), jnp.int32(0)
        for i in range(STEPS):
            here = dest_shard[i] == shard
            slot = jnp.maximum(slot, jnp.where(here, i, 0))
            length = jnp.maximum(length, jnp.where(here, lengths[i], 0))
        slot_of.append(slot)
        tile = jnp.zeros((8, 128), jnp.int32) + length
        if k == BEFORE:
            sizes[k] = tile
        else:
            sizes_out[k] = tile

    def size_copy(k):
        return pltpu.make_async_remote_copy(
            src_ref=sizes_out.at[k],
            dst_ref=sizes.at[k],
            send_sem=size_send.at[k],
            recv_sem=size_recv.at[k],
            device_id=along_dp(k - BEFORE),
            device_id_type=MESH,
        )

    def send_copy(chunk, k):
        return pltpu.make_async_remote_copy(
            src_ref=outbox.at[chunk, k],
            dst_ref=inbox.at[chunk, pl.ds(k * SLOT, SLOT)],
            send_sem=send_sem.at[chunk, k],
            recv_sem=recv_sem.at[chunk, k],
            device_id=along_dp(k - BEFORE),
            device_id_type=MESH,
        )

    def first_copy(chunk, part, k):
        return pltpu.make_async_remote_copy(
            src_ref=outbox.at[chunk, k, :, COLUMNS[part]],
            dst_ref=inbox.at[chunk, pl.ds(k * SLOT, SLOT), COLUMNS[part]],
            send_sem=first_send.at[chunk, part, k],
            recv_sem=first_recv.at[chunk, part, k],
            device_id=along_dp(k - BEFORE),
            device_id_type=MESH,
        )

    others = [k for k in range(STEPS) if k != BEFORE]

    def order_slots(chunk, load):
        for k in range(STEPS):
            if k == BEFORE:
                inbox[chunk, k * SLOT : (k + 1) * SLOT, :] = load(slot_of[k])
            else:
                outbox[chunk, k] = load(slot_of[k])

    slot_copy(0).wait()
    order_slots(0, lambda slot: first_slots[slot])

    pl.semaphore_wait(barrier, len(peers))

    for k in others:
        size_copy(k).start()
    for part in range(2):
        for k in others:
            first_copy(0, part, k).start()
    for chunk in range(1, CHUNKS):
        slot_copy(chunk).wait()

    def send_chunk(chunk, carry):
        order_slots(chunk, lambda slot: slots[chunk - 1, slot])
        for k in others:
            send_copy(chunk, k).start()
        return carry

    for chunk in range(1, SPLIT):
        order_slots(chunk, lambda slot: slots[chunk - 1, slot])
        for part in range(2):
            for k in others:
                first_copy(chunk, part, k).start()
    lax.fori_loop(SPLIT, CHUNKS, send_chunk, 0)

    total[...] = jnp.zeros_like(total)
    squares[...] = jnp.zeros_like(squares)
    head_terms[...] = jnp.zeros_like(head_terms)
    key_rot[0:SLOT, :] = jnp.zeros((SLOT, HD), BF16)
    value_rows[0:SLOT, :] = jnp.zeros((SLOT, HD), BF16)

    for k in others:
        size_copy(k).wait_recv()
    size = [sizes[k, 0:1, :] for k in range(STEPS)]
    offset = [jnp.zeros_like(size[0])]
    for k in range(1, STEPS):
        offset.append(offset[-1] + size[k - 1])

    def step_start(row):
        start = jnp.zeros_like(row)
        for k in range(1, STEPS):
            start = jnp.where(row >= offset[k], offset[k], start)
        return start

    packed_row = lax.broadcasted_iota(jnp.int32, (PACK, 128), 0)
    for block in range(STEPS * SLOT // 128):
        column = lax.broadcasted_iota(jnp.int32, (1, 128), 1) + block * 128
        target = jnp.zeros_like(column)
        for k in range(block * 128 // SLOT, (block * 128 + 127) // SLOT + 1):
            position = column - k * SLOT
            row = jnp.where(position < size[k], offset[k] + position, -1)
            target = jnp.where(position >= 0, row, target)
        select[:, block * 128 : (block + 1) * 128] = jnp.where(packed_row == target, 1.0, 0.0).astype(BF16)

    def ring_copy(way, chunk):
        return pltpu.make_async_remote_copy(
            src_ref=rows.at[0, chunk],
            dst_ref=rows.at[1 + way, chunk],
            send_sem=ring_send.at[way, chunk],
            recv_sem=ring_recv.at[way, chunk],
            device_id=along_mp(1 - 2 * way),
            device_id_type=MESH,
        )

    def first_ring(chunk, part, way):
        return pltpu.make_async_remote_copy(
            src_ref=rows.at[0, chunk, :, COLUMNS[part]],
            dst_ref=rows.at[1 + way, chunk, :, COLUMNS[part]],
            send_sem=early_send.at[chunk, part, way],
            recv_sem=early_recv.at[chunk, part, way],
            device_id=along_mp(1 - 2 * way),
            device_id_type=MESH,
        )

    def pass_copy(way, chunk):
        half = pl.ds(way * HALF, HALF)
        return pltpu.make_async_remote_copy(
            src_ref=rows.at[1 + way, chunk, half],
            dst_ref=rows.at[3, chunk, half],
            send_sem=pass_send.at[way, chunk],
            recv_sem=pass_recv.at[way, chunk],
            device_id=along_mp(1 - 2 * way),
            device_id_type=MESH,
        )

    def pack(chunk, columns=slice(0, WIDTH)):
        packed = jnp.dot(select[...], inbox[chunk, :, columns], preferred_element_type=F32)
        rows[0, chunk, :, columns] = packed.astype(BF16)

    def first_pack(chunk):
        for part in range(2):
            for k in others:
                first_copy(chunk, part, k).wait_recv()
            pack(chunk, COLUMNS[part])
            for way in range(2):
                first_ring(chunk, part, way).start()

    def head_term(chunk):
        parts = thirds(wide_row(value_head, chunk))
        sub = lax.broadcasted_iota(jnp.int32, (8, WIDTH), 0)
        stacked = jnp.zeros((8, WIDTH), F32)
        for i, part in enumerate(parts):
            stacked = jnp.where(sub == i, part.astype(F32), stacked)
        head_terms[...] += dot_last(stacked.astype(BF16), rows[0, chunk])

    def project(source, plane, chunk):
        block = plane * CHUNKS + chunk
        x = rows[source, chunk].astype(F32)
        squared = x * x
        squares[...] += squared[:, :128] + squared[:, 128:]
        scaled = (x * wide_row(gain, block)).astype(BF16)
        for n in range(COLS // WIDTH):
            columns = slice(n * WIDTH, (n + 1) * WIDTH)
            total[:, columns] += jnp.dot(
                scaled, weights[block, :, columns], preferred_element_type=F32
            )

    first_pack(0)

    for copy in small_copies:
        copy.wait()

    half_sign = jnp.where(lax.broadcasted_iota(jnp.int32, (TILE, TILE), 1) < HD // 2, -1.0, 1.0)
    for b in range(TILES):
        at = slice(b * TILE, (b + 1) * TILE)
        row = lax.broadcasted_iota(jnp.int32, (TILE, TILE), 0) + b * TILE
        angle = (row - step_start(row)).astype(F32) * frequency[...]
        cosines[at, :] = jnp.cos(angle)
        sines[at, :] = jnp.sin(angle) * half_sign

    for copy in weight_copies:
        copy.wait()

    def near(t):
        for way in range(2):
            pass_copy(way, t).start()

        def one(source, inner):
            project(source, lax.rem(mp + 2 * source - 3 + PLANES, PLANES), t)
            return inner

        lax.fori_loop(1, 3, one, 0)

    first_pack(1)
    head_term(0)
    project(0, mp, 0)
    for part in range(2):
        for way in range(2):
            first_ring(0, part, way).wait_recv()
    near(0)

    def advance(t, carry):
        @pl.when(t + 1 < CHUNKS)
        def _():
            for k in others:
                send_copy(t + 1, k).wait_recv()
            pack(t + 1)
            for way in range(2):
                ring_copy(way, t + 1).start()

        @pl.when(t < CHUNKS)
        def _():
            head_term(t)
            project(0, mp, t)

            @pl.when(t == 1)
            def _():
                for part in range(2):
                    for way in range(2):
                        first_ring(1, part, way).wait_recv()

            @pl.when(t >= SPLIT)
            def _():
                for way in range(2):
                    ring_copy(way, t).wait_recv()

            near(t)

        for way in range(2):
            pass_copy(way, t - 1).wait_recv()
        project(3, lax.rem(mp + 2, PLANES), t - 1)
        return carry

    lax.fori_loop(1, CHUNKS + 1, advance, 0)

    query_scale = math.log2(math.e) / math.sqrt(HD)

    def rotate(b):
        at = slice(b * TILE, (b + 1) * TILE)
        below = slice(SLOT + b * TILE, SLOT + (b + 1) * TILE)
        mean = jnp.sum(squares[at, :], axis=1, keepdims=True) / (PLANES * CHUNKS * WIDTH)
        scale = lax.rsqrt(mean + EPSILON)
        cosine, sine = cosines[at, :], sines[at, :]

        def turned(head):
            x = total[at, head * HD : (head + 1) * HD] * scale
            return x * cosine + pltpu.roll(x, HD // 2, 1) * sine

        for head in range(HEADS):
            query_rot[b, head * TILE : (head + 1) * TILE, :] = (turned(head) * query_scale).astype(BF16)
        key_rot[below, :] = turned(HEADS).astype(BF16)
        value_rows[below, :] = (total[at, (HEADS + 1) * HD :] * scale).astype(BF16)

    folded = jnp.concatenate([part.astype(F32) for part in thirds(folded_head[...])], axis=0).astype(BF16)
    reach = lax.broadcasted_iota(jnp.int32, (BAND, TILE), 0) - SLOT
    query_at = lax.broadcasted_iota(jnp.int32, (BAND, TILE), 1)
    lane = lax.broadcasted_iota(jnp.int32, (1, TILE), 1)
    step_sub = lax.broadcasted_iota(jnp.int32, (STEPS, TILE), 0)
    time_sub = lax.broadcasted_iota(jnp.int32, (LANES, TILE), 0)

    def attend(b):
        band = slice(b * TILE, b * TILE + BAND)
        keys = key_rot[band, :]
        row = lane + b * TILE
        start = step_start(row)
        step_row = jnp.zeros_like(row)
        for k in range(1, STEPS):
            step_row = step_row + jnp.where(row >= offset[k], 1, 0)
        position_row = row - start
        allowed = (reach <= query_at) & (reach >= start - b * TILE)
        lifted = lifted_all[:, band]
        head_weights = []
        for head in range(HEADS):
            scores = dot_last(keys, query_rot[b, head * TILE : (head + 1) * TILE, :])
            scores = jnp.where(allowed, scores, -1e30)
            peak = jnp.max(scores, axis=0, keepdims=True)
            head_weights.append(jnp.exp2(scores - peak).astype(BF16))
        sums = jnp.dot(lifted, jnp.concatenate(head_weights, axis=1), preferred_element_type=F32)
        ends = head_terms[:, b * TILE : (b + 1) * TILE]
        term = ends[0:1] + ends[1:2] + ends[2:3]
        for head in range(HEADS):
            part = slice(head * TILE, (head + 1) * TILE)
            above = sums[head : head + 1, part] + sums[HEADS + head : HEADS + head + 1, part]
            term = term + above / sums[2 * HEADS : 2 * HEADS + 1, part]
        spread = jnp.where(step_sub == step_row, term, 0.0)
        spread = jnp.concatenate([part.astype(F32) for part in thirds(spread)], axis=0).astype(BF16)
        placed = jnp.where(time_sub == position_row, 1.0, 0.0).astype(BF16)
        return sum_of_thirds(dot_last(spread, placed))

    for b in range(TILES):
        rotate(b)
    through = sum_of_thirds(dot_last(folded, value_rows[...]))
    high, low, _ = thirds(through)
    lifted_all = jnp.concatenate(
        [high.astype(F32), low.astype(F32), jnp.ones((HEADS, SLOT + PACK), F32)], axis=0
    ).astype(BF16)
    shares = attend(0)
    for b in range(1, TILES):
        shares = shares + attend(b)

    def back_copy(by, k, plane):
        return pltpu.make_async_remote_copy(
            src_ref=by_step.at[k],
            dst_ref=arrived.at[plane, k],
            send_sem=back_send.at[by, k],
            recv_sem=back_recv.at[by, k],
            device_id=(along_dp(BEFORE - k)[0], along_mp(by)[1]),
            device_id_type=MESH,
        )

    remote = [(by, k) for k in range(STEPS) for by in range(PLANES) if by or k != BEFORE]
    for k in range(STEPS):
        for half in range(LANES // 128):
            by_step[k, half : half + 1, :] = shares[k : k + 1, half * 128 : (half + 1) * 128]
    for by, k in remote:
        back_copy(by, k, mp).start()
    arrived[mp, BEFORE] = by_step[BEFORE]
    padded_rewards[...] = jnp.zeros_like(padded_rewards)
    padded_rewards[:, 0:SLOT] = rewards[...]
    for by, k in remote:
        back_copy(by, k, along_mp(-by)[1]).wait_recv()

    sub = lax.broadcasted_iota(jnp.int32, (STEPS, LANES), 0)
    time = lax.broadcasted_iota(jnp.int32, (STEPS, LANES), 1)
    slot_values = jnp.zeros((STEPS, LANES), F32)
    length = jnp.zeros((STEPS, LANES), jnp.int32)
    for i in range(STEPS):
        step = jnp.minimum(lax.rem(dest_shard[i] - dp + SHARDS, SHARDS), STEPS - 1)
        both = (arrived[0, step] + arrived[1, step]) + (arrived[2, step] + arrived[3, step])
        line = jnp.concatenate([both[0:1], both[1:2]], axis=1)
        slot_values = jnp.where(sub == i, line, slot_values)
        length = jnp.where(sub == i, lengths[i], length)
    live = time < length
    values = jnp.where(live, slot_values, 0.0)
    following = jnp.where(time + 1 < length, pltpu.roll(values, LANES - 1, 1), 0.0)
    advantages = jnp.where(live, padded_rewards[...] + DISCOUNT * following - values, 0.0)
    shift = 1
    while shift < SLOT:
        later = jnp.where(time < LANES - shift, pltpu.roll(advantages, LANES - shift, 1), 0.0)
        advantages = advantages + (DISCOUNT * SMOOTHING) ** shift * later
        shift *= 2
    both_out[0:STEPS, :] = values
    both_out[STEPS:, :] = advantages

    for k in others:
        size_copy(k).wait_send()

    for chunk in range(SPLIT):
        for part in range(2):
            for k in others:
                first_copy(chunk, part, k).wait_send()
            for way in range(2):
                first_ring(chunk, part, way).wait_send()

    def drain(chunk, carry):
        for way in range(2):
            pass_copy(way, chunk).wait_send()

        @pl.when(chunk >= SPLIT)
        def _():
            for k in others:
                send_copy(chunk, k).wait_send()
            for way in range(2):
                ring_copy(way, chunk).wait_send()

        return carry

    lax.fori_loop(0, CHUNKS, drain, 0)
    for by, k in remote:
        back_copy(by, k, mp).wait_send()


def local(
    hidden,
    rewards,
    lengths,
    dest_shard,
    source_owner,
    pack_offset,
    segment_ids,
    norm_gain,
    w_query,
    w_key,
    w_value,
    value_head,
    folded_head,
):
    blocks = PLANES * CHUNKS
    half = HD // 2
    frequency = (ROPE_BASE ** (-np.arange(half, dtype=np.float64) / half)).astype(np.float32)
    frequency = jnp.asarray(np.concatenate([frequency, frequency])[None, :])
    smem = pl.BlockSpec(memory_space=pltpu.SMEM)
    vmem = pl.BlockSpec(memory_space=pltpu.VMEM)
    hbm = pl.BlockSpec(memory_space=pl.ANY)
    dma = pltpu.SemaphoreType.DMA
    both = pl.pallas_call(
        kernel,
        name="critic",
        out_shape=jax.ShapeDtypeStruct((2 * STEPS, LANES), F32),
        in_specs=[smem] * 2 + [hbm] * 9,
        out_specs=vmem,
        scratch_shapes=[
            pltpu.VMEM((2 * blocks, 128), F32),
            pltpu.VMEM((2 * CHUNKS, 128), F32),
            pltpu.VMEM((HEADS, HD), F32),
            pltpu.VMEM((1, HD), F32),
            pltpu.VMEM((STEPS, SLOT), F32),
            pltpu.VMEM((STEPS, SLOT, WIDTH), BF16),
            pltpu.VMEM((CHUNKS - 1, STEPS, SLOT, WIDTH), BF16),
            pltpu.VMEM((CHUNKS, STEPS, SLOT, WIDTH), BF16),
            pltpu.VMEM((CHUNKS, STEPS * SLOT, WIDTH), BF16),
            pltpu.VMEM((blocks, WIDTH, COLS), BF16),
            pltpu.VMEM((PLANES, CHUNKS, PACK, WIDTH), BF16),
            pltpu.VMEM((PACK, COLS), F32),
            pltpu.VMEM((PACK, 128), F32),
            pltpu.VMEM((8, PACK), F32),
            pltpu.VMEM((PACK, STEPS * SLOT), BF16),
            pltpu.VMEM((PACK, HD), F32),
            pltpu.VMEM((PACK, HD), F32),
            pltpu.VMEM((STEPS, 8, 128), jnp.int32),
            pltpu.VMEM((STEPS, 8, 128), jnp.int32),
            pltpu.VMEM((TILES, HEADS * TILE, HD), BF16),
            pltpu.VMEM((SLOT + PACK, HD), BF16),
            pltpu.VMEM((SLOT + PACK, HD), BF16),
            pltpu.VMEM((STEPS, LANES // 128, 128), F32),
            pltpu.VMEM((PLANES, STEPS, LANES // 128, 128), F32),
            pltpu.VMEM((STEPS, LANES), F32),
            dma((5,)),
            dma((CHUNKS,)),
            dma((3,)),
            dma((STEPS,)),
            dma((STEPS,)),
            dma((SPLIT, 2, STEPS)),
            dma((SPLIT, 2, STEPS)),
            dma((SPLIT, 2, 2)),
            dma((SPLIT, 2, 2)),
            dma((CHUNKS, STEPS)),
            dma((CHUNKS, STEPS)),
            dma((2, CHUNKS)),
            dma((2, CHUNKS)),
            dma((2, CHUNKS)),
            dma((2, CHUNKS)),
            dma((PLANES, STEPS)),
            dma((PLANES, STEPS)),
        ],
        compiler_params=pltpu.CompilerParams(
            collective_id=0, has_side_effects=True, vmem_limit_bytes=67_043_328
        ),
    )(
        lengths,
        dest_shard,
        norm_gain.reshape(2 * blocks, 128),
        value_head.reshape(2 * CHUNKS, 128),
        folded_head.reshape(HEADS, HD),
        frequency,
        rewards,
        hidden.reshape(STEPS, SLOT, CHUNKS * WIDTH),
        w_query.reshape(blocks, WIDTH, HEADS * HD),
        w_key.reshape(blocks, WIDTH, HD),
        w_value.reshape(blocks, WIDTH, HD),
    )
    return both[:STEPS, :SLOT], both[STEPS:, :SLOT]


def solution(mesh):
    return jax.shard_map(
        local,
        mesh=mesh,
        in_specs=(
            P("dp", "mp"),
            P("dp", None),
            P("dp"),
            P("dp"),
            P("dp"),
            P("dp"),
            P("dp"),
            P(),
            P(None, "mp"),
            P(None, "mp"),
            P(None, "mp"),
            P("mp"),
            P("mp"),
        ),
        out_specs=(P("dp", None), P("dp", None)),
        check_vma=False,
    )
```
